32 devices in a mesh: grp: 2 (over core), gx: 4 (over z), gy: 4 (over y, x).
Axes of the slice: x: 2, y: 2, z: 4, core: 2. Of those that a mesh axis runs over, the one named last changes fastest.
Arguments:
- gas_velocity: float32 [3, 64, 128, 384], P(None, 'gx', ('grp', 'gy')), may hold values from -6 to 6
- parcel_z: float32 [3072, 256], P(('grp', 'gx', 'gy')), may hold values from 0 to 383
- parcel_velocity: float32 [3072, 3, 256], P(('grp', 'gx', 'gy')), may hold values from -6 to 6
- parcel_rate: float32 [3072, 256], P(('grp', 'gx', 'gy')), may hold values from 0.05 to 5
- parcel_mass: float32 [3072, 256], P(('grp', 'gx', 'gy')), may hold values from 0.2 to 2
- parcel_column: int32 [3072], P(('grp', 'gx', 'gy')), may hold values from 0 to 8191, as said below
Outputs:
- gas_out: float32 [3, 64, 128, 384], P(None, 'gx', ('grp', 'gy'))
- parcel_out: float32 [6144, 3, 256], P(('grp', 'gx', 'gy'))
The draws below stay inside these ranges and needn't reach their ends.
Inputs may be any that keep to these rules, and one draw needn't show every extreme that they name: `parcel_column`: each block's column lies in its own device's cells or in those of one of its four face neighbours along the first and second dimensions (cycles of 4 and 8 slabs). One device sends at most 24 blocks to one neighbour; in every draw some device keeps all its blocks and receives 24 blocks from each of its four neighbours.
All inputs are finite; a program needn't handle non-finite values.
Results may differ from the reference program's by a relative error of at most 0.0003.
Values sent between devices are 32-bit elements; how exact they have to be, the bound alone decides.
No kernel may reach another device: no remote copies, remote signals or barrier semaphores. Data moves between devices by JAX's collectives and lax.ppermute only.
A program may use at most 64 MiB of HBM per device.

```python
import math
import jax
import jax.numpy as jnp
from jax import lax

CX = 16
CY = 16
NZ = 384
SLOT_DEV = 96
BLK = 256
ITERS = 2
MIG = 24
XSLABS = 4
YINNER = 4
YSLABS = 8
NX = 64
NY = 128
NBLK = 3072
NBLK_OUT = 6144


def place_of_drawn(device):
    group = device // (XSLABS * YINNER)
    return (device // YINNER % XSLABS, group * YINNER + device % YINNER)


def device_at_drawn(x_slab, y_slab):
    x_slab = x_slab % XSLABS
    y_slab = y_slab % YSLABS
    return y_slab // YINNER * XSLABS * YINNER + x_slab * YINNER + y_slab % YINNER


def shuffle(slot_key):
    return jax.random.permutation(slot_key, SLOT_DEV)


def draw_parcel_column(key, part):
    count_dev = XSLABS * YSLABS
    keys = jax.random.split(jax.random.fold_in(key, 7), 5)
    counts = jax.random.randint(keys[0], (count_dev, 4), 0, MIG + 1)
    chosen = jax.random.randint(keys[1], (), 0, count_dev)
    device = jnp.arange(count_dev, dtype=jnp.int32)
    counts = jnp.where(device[:, None] == chosen, 0, counts)
    x_chosen, y_chosen = place_of_drawn(chosen)
    sources = jnp.stack([device_at_drawn(x_chosen - 1, y_chosen), device_at_drawn(x_chosen + 1, y_chosen), device_at_drawn(x_chosen, y_chosen - 1), device_at_drawn(x_chosen, y_chosen + 1)])
    counts = counts.at[sources, jnp.arange(4)].set(MIG)
    bounds = jnp.cumsum(counts, 1)
    slot = jnp.arange(SLOT_DEV)[None, :]
    direction = jnp.where(slot < bounds[:, 0:1], 1, jnp.where(slot < bounds[:, 1:2], 2, jnp.where(slot < bounds[:, 2:3], 3, jnp.where(slot < bounds[:, 3:4], 4, 0))))
    orders = jax.vmap(shuffle)(jax.random.split(keys[2], count_dev))
    direction = jnp.take_along_axis(direction, orders, 1)
    x_all, y_all = place_of_drawn(device)
    step_x = (direction == 1).astype(jnp.int32) - (direction == 2).astype(jnp.int32)
    step_y = (direction == 3).astype(jnp.int32) - (direction == 4).astype(jnp.int32)
    target_x = (x_all[:, None] + step_x) % XSLABS
    target_y = (y_all[:, None] + step_y) % YSLABS
    cell_x = target_x * CX + jax.random.randint(keys[3], (count_dev, SLOT_DEV), 0, CX)
    cell_y = target_y * CY + jax.random.randint(keys[4], (count_dev, SLOT_DEV), 0, CY)
    return (cell_x * NY + cell_y).reshape(-1).astype(jnp.int32)


def levels(rng, shape, cuts, least, largest):
    def one(dim, parts):
        heights = jax.random.uniform(jax.random.fold_in(jax.random.fold_in(rng, 6), dim), (parts,), jnp.float32, least / len(cuts), largest / len(cuts))
        return jnp.repeat(jnp.exp(heights), shape[dim] // parts).reshape((-1,) + (1,) * (len(shape) - dim - 1))

    gain = one(*cuts[0])
    for cut in cuts[1:]:
        gain = gain * one(*cut)
    return gain


def gaussian(stream_key, shape, deviation, reach, pieces=(), held_as=jnp.bfloat16):
    result = jax.random.normal(stream_key, shape, jnp.float32) * deviation
    if len(pieces) > 0:
        result = levels(stream_key, shape, pieces, -0.22, 0.18) * result
    return jnp.clip(result, min=-reach, max=reach).astype(held_as)


def setup_inputs(seed: int = 0) -> dict:
    streams_of = jax.random.split(jax.random.key(seed), 7)
    gas_velocity = gaussian(streams_of[0], (3, NX, NY, NZ), 1.0, 6.0, ((1, 4), (2, 8)), jnp.float32)
    parcel_z = jnp.clip(383.0 * jax.random.uniform(streams_of[1], (NBLK, BLK), jnp.float32) ** levels(streams_of[1], (NBLK, BLK), ((0, 32),), -0.2, 0.2), 0.0, 383.0)
    parcel_velocity = gaussian(streams_of[2], (NBLK, 3, BLK), 1.0, 6.0, ((0, 32),), jnp.float32)
    parcel_rate = jnp.clip(jnp.exp(math.log(5.0) - 4.6051702 * jax.random.uniform(streams_of[3], (NBLK, BLK), jnp.float32) ** levels(streams_of[3], (NBLK, BLK), ((0, 32),), -0.2, 0.2)), 0.05, 5.0)
    parcel_mass = jnp.clip(jnp.exp(math.log(2.0) - 2.3025851 * jax.random.uniform(streams_of[4], (NBLK, BLK), jnp.float32) ** levels(streams_of[4], (NBLK, BLK), ((0, 32),), -0.2, 0.2)), 0.2, 2.0)
    parcel_column = draw_parcel_column(jax.random.fold_in(streams_of[6], 71), 0)
    return {"gas_velocity": gas_velocity, "parcel_z": parcel_z, "parcel_velocity": parcel_velocity, "parcel_rate": parcel_rate, "parcel_mass": parcel_mass, "parcel_column": parcel_column}


NU = 0.1


def diffuse(field):
    beside = jnp.roll(field, -1, 1) + jnp.roll(field, 1, 1) + jnp.roll(field, -1, 2) + jnp.roll(field, 1, 2)
    zeros_plane = jnp.zeros_like(field[..., :1])
    z_above = jnp.concatenate([field[..., 1:], zeros_plane], -1)
    z_below = jnp.concatenate([zeros_plane, field[..., :-1]], -1)
    return field + NU * (beside + z_above + z_below - 6.0 * field)


def place_of(device):
    group = device // (XSLABS * YINNER)
    return (device // YINNER) % XSLABS, group * YINNER + device % YINNER


def device_at(x_slab, y_slab):
    x_slab = x_slab % XSLABS
    y_slab = y_slab % YSLABS
    return (y_slab // YINNER) * XSLABS * YINNER + x_slab * YINNER + y_slab % YINNER


def heading(column, x_index, y_index):
    target_x = (column // NY) // CX
    target_y = (column % NY) // CY
    return jnp.where(target_x == (x_index + 1) % XSLABS, 1,
                     jnp.where(target_x == (x_index - 1) % XSLABS, 2,
                               jnp.where(target_y == (y_index + 1) % YSLABS, 3,
                                         jnp.where(target_y == (y_index - 1) % YSLABS, 4, 0)))).astype(jnp.int32)


def pack(state, direction):
    slots = state.shape[0]
    flat = state.reshape(slots, -1)
    staying = state * (direction == 0).astype(jnp.float32)[:, None, None]
    chosen = jnp.stack([(direction == code).astype(jnp.int32) for code in range(1, 5)])
    position = jnp.cumsum(chosen, 1) - 1
    select = ((chosen[:, None, :] == 1) & (position[:, None, :] == jnp.arange(MIG, dtype=jnp.int32)[None, :, None])).astype(jnp.float32)
    outbox = jnp.einsum('cms,sk->cmk', select, flat, precision=lax.Precision.HIGHEST)
    return staying, outbox.reshape(4, MIG, state.shape[1], state.shape[2])


def reference(gas_velocity, parcel_z, parcel_velocity, parcel_rate, parcel_mass, parcel_column):
    field = gas_velocity
    for substep in range(ITERS):
        field = diffuse(field)
    count_dev = XSLABS * YSLABS
    column_f = parcel_column.astype(jnp.float32)
    state = jnp.concatenate([parcel_z[:, None, :], parcel_velocity, parcel_rate[:, None, :], parcel_mass[:, None, :],
                             jnp.broadcast_to(column_f[:, None, None], (NBLK, 1, BLK))], 1)
    state = state.reshape(count_dev, SLOT_DEV, 7, BLK)
    device = jnp.arange(count_dev, dtype=jnp.int32)
    x_all, y_all = place_of(device)
    direction = jax.vmap(heading)(parcel_column.reshape(count_dev, SLOT_DEV), x_all[:, None], y_all[:, None])
    staying, outbox = jax.vmap(pack)(state, direction)
    sources = jnp.stack([device_at(x_all - 1, y_all), device_at(x_all + 1, y_all),
                         device_at(x_all, y_all - 1), device_at(x_all, y_all + 1)], 1)
    arrivals = outbox[sources, jnp.arange(4, dtype=jnp.int32)[None, :]]
    slotted = jnp.concatenate([staying, arrivals.reshape(count_dev, 4 * MIG, 7, BLK)], 1).reshape(NBLK_OUT, 7, BLK)
    positions = slotted[:, 0]
    velocity = jnp.moveaxis(slotted[:, 1:4], 1, 0)
    rates = slotted[:, 4]
    masses = slotted[:, 5]
    column = slotted[:, 6, 0].astype(jnp.int32)
    cell_low = jnp.minimum(jnp.floor(positions).astype(jnp.int32), NZ - 2)
    fraction = positions - cell_low.astype(jnp.float32)
    column_rows = jnp.broadcast_to(column[:, None], cell_low.shape)
    lines = field.reshape(3, NX * NY, NZ)
    value_low = lines[:, column_rows, cell_low]
    value_high = lines[:, column_rows, cell_low + 1]
    gas_at = value_low * (1.0 - fraction) + value_high * fraction
    relax = rates / (1.0 + rates)
    updated = velocity + relax * (gas_at - velocity)
    momentum = masses * (velocity - updated)
    source = jnp.zeros((3, NX * NY, NZ), jnp.float32)
    source = source.at[:, column_rows, cell_low].add(momentum * (1.0 - fraction))
    source = source.at[:, column_rows, cell_low + 1].add(momentum * fraction)
    gas_out = (lines + source).reshape(3, NX, NY, NZ)
    return gas_out, jnp.moveaxis(updated, 0, 1)
```

```python
import functools

import jax
import jax.numpy as jnp
from jax import lax
from jax.experimental import pallas as pl
from jax.experimental.pallas import tpu as pltpu
from jax.sharding import PartitionSpec as P

ITERS = 2
NU = 0.1
LANES = 128
SUB = 8
Y_AXES = ("grp", "gy")

VMEM = pl.BlockSpec(memory_space=pltpu.VMEM)
SMEM = pl.BlockSpec(memory_space=pltpu.SMEM)
ANY = pl.BlockSpec(memory_space=pl.ANY)


def y_place():
    return lax.axis_index("grp") * lax.axis_size("gy") + lax.axis_index("gy")


def heading_of(column, dims):
    x_count, y_count, cells_x, cells_y = dims
    rows_total = cells_y * y_count
    x_index, y_index = lax.axis_index("gx"), y_place()
    target_x = column // rows_total // cells_x
    target_y = column % rows_total // cells_y
    return jnp.where(
        target_x == (x_index + 1) % x_count,
        1,
        jnp.where(
            target_x == (x_index + x_count - 1) % x_count,
            2,
            jnp.where(
                target_y == (y_index + 1) % y_count,
                3,
                jnp.where(target_y == (y_index + y_count - 1) % y_count, 4, 0),
            ),
        ),
    )


def local_of(column, dims):
    x_count, y_count, cells_x, cells_y = dims
    rows_total = cells_y * y_count
    return column // rows_total % cells_x * cells_y + column % rows_total % cells_y


def faces_kernel(gas, x_up, x_down, y_up, y_down, pp, pm, mp, mm):
    comps, cells_x, cells_y, depth = gas.shape
    x_up[...] = gas[:, cells_x - 2 :]
    x_down[...] = gas[:, :2]
    for c in range(comps):
        for near in range(2):
            for out, y in ((y_up, cells_y - 2 + near), (y_down, near)):
                out[c, near] = gas[c, :, y, :]
        last_x, last_y = cells_x - 1, cells_y - 1
        for out, x, y in (
            (pp, last_x, last_y),
            (pm, last_x, 0),
            (mp, 0, last_y),
            (mm, 0, 0),
        ):
            out[pl.ds(c, 1), :] = gas[c, x, pl.ds(y, 1), :]


def pack_kernel(dims, capacity, columns, z, v, rate, mass, *refs):
    boxes, box = refs[:4], refs[4]
    slots, width = z.shape
    fields = 6
    rows = fields * capacity + SUB
    box[...] = jnp.zeros_like(box)
    lane = lax.broadcasted_iota(jnp.int32, (1, LANES), 1)

    def one(s, counts):
        column = columns[s]
        head = heading_of(column, dims)
        place = jnp.int32(0)
        for code in range(1, 5):
            place = jnp.where(head == code, counts[code - 1], place)
        counts = tuple(
            counts[code - 1] + (head == code).astype(jnp.int32) for code in range(1, 5)
        )
        ok = (head > 0) & (place < capacity)
        base = jnp.where(ok, (head - 1) * rows, 4 * rows)
        place = jnp.where(ok, place, 0)
        at = base + place
        box[pl.ds(at, 1), :] = z[pl.ds(s, 1), :]
        for c in range(3):
            box[pl.ds(at + (1 + c) * capacity, 1), :] = v[c, pl.ds(s, 1), :]
        box[pl.ds(at + 4 * capacity, 1), :] = rate[pl.ds(s, 1), :]
        box[pl.ds(at + 5 * capacity, 1), :] = mass[pl.ds(s, 1), :]
        tail = base + fields * capacity
        tail = pl.multiple_of(tail, SUB)
        kept = box[pl.ds(tail, 1), pl.ds(0, LANES)]
        box[pl.ds(tail, 1), pl.ds(0, LANES)] = jnp.where(
            lane == place, column.astype(jnp.float32), kept
        )
        return counts

    lax.fori_loop(0, slots, one, (jnp.int32(0),) * 4)
    for code in range(4):
        boxes[code][...] = box[code * rows : (code + 1) * rows, :]


def up_down(value):
    depth = value.shape[-1]
    axis = value.ndim - 1
    level = lax.broadcasted_iota(jnp.int32, value.shape, axis)
    above = jnp.where(level == depth - 1, 0.0, pltpu.roll(value, depth - 1, axis))
    below = jnp.where(level == 0, 0.0, pltpu.roll(value, 1, axis))
    return above + below


def couple_kernel(
    dims,
    capacity,
    columns,
    gas,
    x_low,
    x_high,
    y_low,
    y_high,
    ll,
    lh,
    hl,
    hh,
    z,
    v,
    rate,
    mass,
    in0,
    in1,
    in2,
    in3,
    gas_out,
    parcel_out,
    ext,
    mid,
    lines,
    acc,
    rows_scr,
    weights,
    cells_scr,
    arrived,
    sems,
):
    x_count, y_count, cells_x, cells_y = dims
    comps, _, _, depth = gas.shape
    slots, width = z.shape
    chunks = depth // LANES
    tiles = width // LANES
    top = SUB
    pitch = lines.shape[0] // (cells_x * cells_y)
    acc_pitch = acc.shape[0] // (cells_x * cells_y)
    half = acc_pitch
    inboxes = (in0, in1, in2, in3)

    own = pltpu.make_async_copy(
        gas, ext.at[:, pl.ds(2, cells_x), pl.ds(top, cells_y), :], sems.at[0]
    )
    own.start()
    tails = []
    for code in range(4):
        tail = pltpu.make_async_copy(
            inboxes[code].at[pl.ds(6 * capacity, SUB), pl.ds(0, LANES)],
            arrived.at[pl.ds(code * SUB, SUB), :],
            sems.at[1 + code],
        )
        tail.start()
        tails.append(tail)
    acc[...] = jnp.zeros_like(acc)
    own.wait()

    ext[:, 0:2, top : top + cells_y, :] = x_low[...]
    ext[:, 2 + cells_x : 4 + cells_x, top : top + cells_y, :] = x_high[...]
    for c in range(comps):
        ext[c, 2 : 2 + cells_x, top - 1, :] = y_low[c, 1]
        ext[c, 2 : 2 + cells_x, top + cells_y, :] = y_high[c, 0]
        for corner, x, y in (
            (ll, 1, top - 1),
            (lh, 1, top + cells_y),
            (hl, 2 + cells_x, top - 1),
            (hh, 2 + cells_x, top + cells_y),
        ):
            ext[c, x, pl.ds(y, 1), :] = corner[pl.ds(c, 1), :]

    def first_plane(i, carry):
        x = 1 + i
        for c in range(comps):
            center = ext[c, x, pl.ds(top, cells_y), :]
            beside = (
                ext[c, x + 1, pl.ds(top, cells_y), :]
                + ext[c, x - 1, pl.ds(top, cells_y), :]
                + ext[c, x, pl.ds(top + 1, cells_y), :]
                + ext[c, x, pl.ds(top - 1, cells_y), :]
            )
            mid[c, i, pl.ds(top, cells_y), :] = center + NU * (
                beside + up_down(center) - 6.0 * center
            )
        return carry

    lax.fori_loop(0, cells_x + 2, first_plane, 0)

    x_row = lax.broadcasted_iota(jnp.int32, (cells_x, depth), 0)
    for c in range(comps):
        for face, near, far, inner, low_c, high_c, row in (
            (y_low, 1, 0, top, ll, hl, top - 1),
            (y_high, 0, 1, top + cells_y - 1, lh, hh, top + cells_y),
        ):
            center = face[c, near]
            left = jnp.where(
                x_row == 0, low_c[pl.ds(c, 1), :], pltpu.roll(center, 1, 0)
            )
            right = jnp.where(
                x_row == cells_x - 1,
                high_c[pl.ds(c, 1), :],
                pltpu.roll(center, cells_x - 1, 0),
            )
            inside = ext[c, 2 : 2 + cells_x, inner, :]
            beside = left + right + face[c, far] + inside
            mid[c, 1 : 1 + cells_x, row, :] = center + NU * (
                beside + up_down(center) - 6.0 * center
            )

    def second_plane(i, carry):
        x = 1 + i
        for c in range(comps):
            center = mid[c, x, pl.ds(top, cells_y), :]
            beside = (
                mid[c, x + 1, pl.ds(top, cells_y), :]
                + mid[c, x - 1, pl.ds(top, cells_y), :]
                + mid[c, x, pl.ds(top + 1, cells_y), :]
                + mid[c, x, pl.ds(top - 1, cells_y), :]
            )
            field = center + NU * (beside + up_down(center) - 6.0 * center)
            for h in range(chunks):
                part = field[:, h * LANES : (h + 1) * LANES]
                row = c * chunks + h
                lines[pl.ds(i * cells_y * pitch + row, cells_y, stride=pitch), :] = part
                acc[
                    pl.ds(i * cells_y * acc_pitch + row, cells_y, stride=acc_pitch), :
                ] = part
        return carry

    lax.fori_loop(0, cells_x, second_plane, 0)

    lane = lax.broadcasted_iota(jnp.int32, (LANES, LANES), 0)

    def group(zz, vv, rr, mm, local, out_row):
        for b in range(SUB):
            rows_scr[b * pitch : (b + 1) * pitch, :] = lines[
                pl.ds(pl.multiple_of(local[b] * pitch, SUB), pitch), :
            ]
        gas_rows = [
            [
                rows_scr[pl.ds(c * chunks + h, SUB, stride=pitch), :]
                for h in range(chunks)
            ]
            for c in range(comps)
        ]
        for t in range(tiles):
            part = slice(t * LANES, (t + 1) * LANES)
            pos = zz[:, part]
            low = jnp.minimum(jnp.floor(pos).astype(jnp.int32), depth - 2)
            frac = pos - low.astype(jnp.float32)
            high = low + 1
            low_chunk, low_lane = low >> 7, low & (LANES - 1)
            high_chunk, high_lane = high >> 7, high & (LANES - 1)
            relax = rr[:, part] / (1.0 + rr[:, part])
            cells_scr[:, part] = low_lane
            for c in range(comps):
                at_low = at_high = None
                for h in range(chunks):
                    got_low = jnp.take_along_axis(
                        gas_rows[c][h], low_lane, 1, mode="promise_in_bounds"
                    )
                    got_high = jnp.take_along_axis(
                        gas_rows[c][h], high_lane, 1, mode="promise_in_bounds"
                    )
                    at_low = (
                        got_low if h == 0 else jnp.where(low_chunk == h, got_low, at_low)
                    )
                    at_high = (
                        got_high
                        if h == 0
                        else jnp.where(high_chunk == h, got_high, at_high)
                    )
                gas_at = at_low * (1.0 - frac) + at_high * frac
                vel = vv[c][:, part]
                updated = vel + relax * (gas_at - vel)
                parcel_out[c, pl.ds(out_row, SUB), part] = updated
                momentum = mm[:, part] * (vel - updated)
                for w, share in enumerate((momentum * (1.0 - frac), momentum * frac)):
                    coarse = share.astype(jnp.bfloat16).astype(jnp.float32)
                    fine = share - coarse
                    for h in range(chunks):
                        row = (w * comps + c) * chunks + h
                        here = low_chunk == h
                        weights[t, row * SUB : (row + 1) * SUB, :] = jnp.where(
                            here, coarse, 0.0
                        )
                        row += half
                        weights[t, row * SUB : (row + 1) * SUB, :] = jnp.where(
                            here, fine, 0.0
                        )
        for b in range(SUB):
            spots, shares = [], []
            for t in range(tiles):
                shares.append(
                    weights[t, pl.ds(b, 2 * half, stride=SUB), :].astype(jnp.bfloat16)
                )
                cell = cells_scr[pl.ds(b, 1), t * LANES : (t + 1) * LANES]
                spots.append(
                    jnp.where(lane == cell, 1.0, 0.0).astype(jnp.bfloat16)
                )
            spot = jnp.concatenate(spots, 1)
            lhs = jnp.concatenate(shares, 1)
            both = lax.dot_general(
                lhs, spot, (((1,), (1,)), ((), ())), preferred_element_type=jnp.float32
            )
            at = pl.ds(pl.multiple_of(local[b] * acc_pitch, SUB), acc_pitch)
            acc[at, :] = acc[at, :] + (both[:half] + both[half:])

    weights[...] = jnp.zeros_like(weights)

    sub_row = lax.broadcasted_iota(jnp.int32, (SUB, width), 0)

    def staying(g, carry):
        first = pl.multiple_of(g * SUB, SUB)
        at = pl.ds(first, SUB)
        keep = jnp.zeros((SUB, width), jnp.int32)
        local = []
        for b in range(SUB):
            column = columns[first + b]
            stays = (heading_of(column, dims) == 0).astype(jnp.int32)
            keep = jnp.where(sub_row == b, stays, keep)
            local.append(local_of(column, dims))
        keep = keep == 1
        group(
            z[at, :],
            [jnp.where(keep, v[c, at, :], 0.0) for c in range(3)],
            jnp.where(keep, rate[at, :], 0.0),
            jnp.where(keep, mass[at, :], 0.0),
            local,
            first,
        )
        return carry

    lax.fori_loop(0, slots // SUB, staying, 0)

    for code in range(4):
        tails[code].wait()
        inbox = inboxes[code]

        def arriving(g, carry, code=code, inbox=inbox):
            first = pl.multiple_of(g * SUB, SUB)
            local = [
                local_of(arrived[code * SUB, first + b].astype(jnp.int32), dims)
                for b in range(SUB)
            ]
            field = [
                inbox[pl.ds(pl.multiple_of(first + f * capacity, SUB), SUB), :]
                for f in range(6)
            ]
            group(
                field[0],
                field[1:4],
                field[4],
                field[5],
                local,
                pl.multiple_of(slots + code * capacity + first, SUB),
            )
            return carry

        lax.fori_loop(0, capacity // SUB, arriving, 0)

    lane_row = lax.broadcasted_iota(jnp.int32, (cells_y, LANES), 1)

    def finish(i, carry):
        for c in range(comps):
            before = jnp.zeros((cells_y, LANES), jnp.float32)
            for h in range(chunks):
                row = c * chunks + h
                base = i * cells_y * acc_pitch + row
                low = acc[pl.ds(base, cells_y, stride=acc_pitch), :]
                high = acc[
                    pl.ds(base + comps * chunks, cells_y, stride=acc_pitch), :
                ]
                turned = pltpu.roll(high, 1, 1)
                moved = jnp.where(lane_row == 0, before, turned)
                before = turned
                gas_out[c, i, :, h * LANES : (h + 1) * LANES] = low + moved
        return carry

    lax.fori_loop(0, cells_x, finish, 0)


def neighbour(value, axis, steps):
    count = lax.axis_size(axis)
    pairs = [(source, (source + steps) % count) for source in range(count)]
    return lax.ppermute(value, axis, pairs)


def diagonal(value, x_steps, y_steps):
    groups, x_count, inner = (lax.axis_size(a) for a in ("grp", "gx", "gy"))
    y_count = groups * inner

    def flat(x, y):
        return (y // inner * x_count + x) * inner + y % inner

    pairs = [
        (flat(x, y), flat((x + x_steps) % x_count, (y + y_steps) % y_count))
        for x in range(x_count)
        for y in range(y_count)
    ]
    return lax.ppermute(value, ("grp", "gx", "gy"), pairs)


def body(gas_velocity, parcel_z, parcel_velocity, parcel_rate, parcel_mass, parcel_column):
    f32 = jnp.float32
    comps, cells_x, cells_y, depth = gas_velocity.shape
    slots, width = parcel_z.shape
    capacity = slots // 4
    x_count = lax.axis_size("gx")
    y_count = lax.axis_size(Y_AXES)
    dims = (x_count, y_count, cells_x, cells_y)
    velocity = jnp.transpose(parcel_velocity, (1, 0, 2))

    x_face = jax.ShapeDtypeStruct((comps, 2, cells_y, depth), f32)
    y_face = jax.ShapeDtypeStruct((comps, 2, cells_x, depth), f32)
    corner = jax.ShapeDtypeStruct((comps, depth), f32)
    x_up, x_down, y_up, y_down, pp, pm, mp, mm = pl.pallas_call(
        faces_kernel,
        out_shape=(x_face, x_face, y_face, y_face, corner, corner, corner, corner),
        in_specs=[VMEM],
        out_specs=(VMEM,) * 8,
        name="faces",
    )(gas_velocity)
    ll = diagonal(pp, 1, 1)
    lh = diagonal(pm, 1, -1)
    hl = diagonal(mp, -1, 1)
    hh = diagonal(mm, -1, -1)
    x_low = neighbour(x_up, "gx", 1)
    x_high = neighbour(x_down, "gx", -1)
    y_low = neighbour(y_up, Y_AXES, 1)
    y_high = neighbour(y_down, Y_AXES, -1)

    rows = 6 * capacity + SUB
    box = jax.ShapeDtypeStruct((rows, width), f32)
    outbox = pl.pallas_call(
        functools.partial(pack_kernel, dims, capacity),
        out_shape=(box,) * 4,
        in_specs=[SMEM] + [VMEM] * 4,
        out_specs=(VMEM,) * 4,
        scratch_shapes=[pltpu.VMEM((5 * rows, width), f32)],
        name="pack",
    )(parcel_column, parcel_z, velocity, parcel_rate, parcel_mass)
    inboxes = [
        neighbour(outbox[0], "gx", 1),
        neighbour(outbox[1], "gx", -1),
        neighbour(outbox[2], Y_AXES, 1),
        neighbour(outbox[3], Y_AXES, -1),
    ]

    chunks = depth // LANES
    cells = cells_x * cells_y
    pitch = -(-comps * chunks // SUB) * SUB
    acc_pitch = -(-2 * comps * chunks // SUB) * SUB
    total = slots + 4 * capacity
    gas_out, updated = pl.pallas_call(
        functools.partial(couple_kernel, dims, capacity),
        out_shape=(
            jax.ShapeDtypeStruct((comps, cells_x, cells_y, depth), f32),
            jax.ShapeDtypeStruct((3, total, width), f32),
        ),
        in_specs=[SMEM, ANY] + [VMEM] * 16,
        out_specs=(VMEM, VMEM),
        scratch_shapes=[
            pltpu.VMEM((comps, cells_x + 4, cells_y + 2 * SUB, depth), f32),
            pltpu.VMEM((comps, cells_x + 2, cells_y + 2 * SUB, depth), f32),
            pltpu.VMEM((cells * pitch, LANES), f32),
            pltpu.VMEM((cells * acc_pitch, LANES), f32),
            pltpu.VMEM((SUB * pitch, LANES), f32),
            pltpu.VMEM((width // LANES, 2 * acc_pitch * SUB, LANES), f32),
            pltpu.VMEM((SUB, width), jnp.int32),
            pltpu.SMEM((4 * SUB, LANES), f32),
            pltpu.SemaphoreType.DMA((5,)),
        ],
        name="couple",
    )(
        parcel_column,
        gas_velocity,
        x_low,
        x_high,
        y_low,
        y_high,
        ll,
        lh,
        hl,
        hh,
        parcel_z,
        velocity,
        parcel_rate,
        parcel_mass,
        *inboxes,
    )
    return gas_out, jnp.transpose(updated, (1, 0, 2))


def solution(mesh):
    placed = (
        P(None, "gx", Y_AXES, None),
        P(("grp", "gx", "gy"), None),
        P(("grp", "gx", "gy"), None, None),
        P(("grp", "gx", "gy"), None),
        P(("grp", "gx", "gy"), None),
        P(("grp", "gx", "gy")),
    )
    return jax.shard_map(
        body,
        mesh=mesh,
        in_specs=placed,
        out_specs=(P(None, "gx", Y_AXES, None), P(("grp", "gx", "gy"), None, None)),
        check_vma=False,
    )
```

```python
import functools

import jax
import jax.numpy as jnp
from jax import lax
from jax.experimental import pallas as pl
from jax.experimental.pallas import tpu as pltpu
from jax.sharding import PartitionSpec as P


NU = 0.1
LANES = 128
SUB = 8
UNROLL = 3
FIELDS = 6
Y_AXES = ("grp", "gy")
F32 = jnp.float32
BF16 = jnp.bfloat16

VMEM = pl.BlockSpec(memory_space=pltpu.VMEM)
SMEM = pl.BlockSpec(memory_space=pltpu.SMEM)
HBM = pl.BlockSpec(memory_space=pltpu.HBM)


def quotient(value, by):
    if by & (by - 1) == 0:
        return value >> (by.bit_length() - 1)
    return lax.div(value, jnp.full_like(value, by))


def remainder(value, by):
    if by & (by - 1) == 0:
        return value & (by - 1)
    return lax.rem(value, jnp.full_like(value, by))


def y_place():
    return lax.axis_index("grp") * lax.axis_size("gy") + lax.axis_index("gy")


def heading_of(column, dims):
    x_count, y_count, cells_x, cells_y = dims
    rows_total = cells_y * y_count
    x_index, y_index = lax.axis_index("gx"), y_place()
    target_x = quotient(column, rows_total * cells_x)
    target_y = quotient(remainder(column, rows_total), cells_y)
    x_up, x_down = lax.rem(x_index + 1, x_count), lax.rem(x_index + x_count - 1, x_count)
    y_up, y_down = lax.rem(y_index + 1, y_count), lax.rem(y_index + y_count - 1, y_count)
    return jnp.where(
        target_x == x_up,
        1,
        jnp.where(
            target_x == x_down,
            2,
            jnp.where(target_y == y_up, 3, jnp.where(target_y == y_down, 4, 0)),
        ),
    )


def local_of(column, dims):
    _, y_count, cells_x, cells_y = dims
    x = remainder(quotient(column, cells_y * y_count), cells_x)
    return x * cells_y + remainder(column, cells_y)


def faces_kernel(gas, z, v, rate, mass, x_up, x_down, y_up, y_down, ext, state, sems):
    comps, cells_x, cells_y, depth = gas.shape
    chunks = depth // LANES
    copies = [
        pltpu.make_async_copy(
            gas.at[:, :, :, pl.ds(h * LANES, LANES)],
            ext.at[:, h, pl.ds(2, cells_x), pl.ds(SUB, cells_y), :],
            sems.at[h],
        )
        for h in range(chunks)
    ]
    for i, (source, target) in enumerate(
        (
            (z, state.at[0]),
            (v, state.at[pl.ds(1, 3)]),
            (rate, state.at[4]),
            (mass, state.at[5]),
        )
    ):
        copies.append(pltpu.make_async_copy(source, target, sems.at[chunks + i]))
    for copy in copies:
        copy.start()
    rows = pl.ds(SUB, cells_y)
    for h in range(chunks):
        copies[h].wait()
        for c in range(comps):
            for near in range(2):
                x_up[c, h, near] = ext[c, h, cells_x + near, rows, :]
                x_down[c, h, near] = ext[c, h, 2 + near, rows, :]
                planes = pl.ds(2, cells_x)
                y_up[c, h, near] = ext[c, h, planes, SUB + cells_y - 2 + near, :]
                y_down[c, h, near] = ext[c, h, planes, SUB + near, :]
    for copy in copies[chunks:]:
        copy.wait()


def pack_kernel(dims, capacity, columns, state, box0, box1, box2, box3, keep):
    boxes = (box0, box1, box2, box3)
    _, slots, _ = state.shape
    column = columns[...]
    head = heading_of(column, dims)
    code = lax.broadcasted_iota(jnp.int32, (SUB, slots), 0) + 1
    leaves = jnp.where((code == head) & (code <= 4), 1.0, 0.0)
    before = jnp.where(
        lax.broadcasted_iota(jnp.int32, (slots, slots), 0)
        < lax.broadcasted_iota(jnp.int32, (slots, slots), 1),
        1.0,
        0.0,
    )
    ranks = jnp.dot(
        leaves.astype(BF16), before.astype(BF16), preferred_element_type=F32
    )
    rank = jnp.sum(ranks * leaves, 0, keepdims=True).astype(jnp.int32)
    target = jnp.where(
        (head > 0) & (rank < capacity), (head - 1) * capacity + rank, -1
    )
    select = jnp.where(
        lax.broadcasted_iota(jnp.int32, (4 * capacity, slots), 0) == target, 1.0, 0.0
    ).astype(BF16)
    for f in range(FIELDS):
        whole = state[f]
        first = whole.astype(BF16)
        rest = whole - first.astype(F32)
        second = rest.astype(BF16)
        third = (rest - second.astype(F32)).astype(BF16)
        moved = (
            jnp.dot(select, first, preferred_element_type=F32)
            + jnp.dot(select, second, preferred_element_type=F32)
        ) + jnp.dot(select, third, preferred_element_type=F32)
        for d in range(4):
            boxes[d][f * capacity : (f + 1) * capacity, :] = moved[
                d * capacity : (d + 1) * capacity
            ]
    digit = lax.broadcasted_iota(jnp.int32, (SUB, slots), 0)
    digits = jnp.where(
        digit == 0,
        column & 255,
        jnp.where(
            digit == 1, (column >> 8) & 255, jnp.where(digit == 2, column >> 16, 0)
        ),
    )
    found = lax.dot_general(
        digits.astype(F32).astype(BF16),
        select,
        (((1,), (1,)), ((), ())),
        preferred_element_type=F32,
    )
    same = lax.broadcasted_iota(jnp.int32, (slots, slots), 0)
    same = same == lax.broadcasted_iota(jnp.int32, (slots, slots), 1)
    keep[...] = jnp.dot(
        jnp.where(same & (head == 0), 1.0, 0.0).astype(BF16),
        jnp.ones((slots, LANES), BF16),
        preferred_element_type=F32,
    )
    tail = found[0:1] + 256.0 * found[1:2] + 65536.0 * found[2:3]
    for d in range(4):
        boxes[d][FIELDS * capacity : FIELDS * capacity + 1, 0 : 4 * capacity] = tail


def relay_kernel(x_low, x_high, box2, box3, up, down, out2, out3):
    del box2, box3, out2, out3
    comps, chunks, _, cells_y, _ = x_low.shape
    for side, (face, near) in enumerate(((x_low, 1), (x_high, 0))):
        for c in range(comps):
            for h in range(chunks):
                row = pl.ds((side * comps + c) * chunks + h, 1)
                up[row, :] = face[c, h, near, pl.ds(cells_y - 1, 1), :]
                down[row, :] = face[c, h, near, pl.ds(0, 1), :]


def stage_one(space, u, zz, vv, rr, mm, local, store):
    lines, rows_scr, shares, marks, comps, chunks = space
    steps = rows_scr.shape[1]
    for b in range(SUB):
        for k in range(steps):
            at = pl.multiple_of((local[b] * steps + k) * SUB, SUB)
            rows_scr[u, k, b * SUB : (b + 1) * SUB, :] = lines[pl.ds(at, SUB), :]
    gas_rows = [
        rows_scr[u, r // SUB, pl.ds(r % SUB, SUB, stride=SUB), :]
        for r in range(comps * chunks)
    ]
    top_cell = chunks * LANES - 2
    for t in range(zz.shape[1] // LANES):
        part = slice(t * LANES, (t + 1) * LANES)
        pos = zz[:, part]
        low = jnp.minimum(jnp.floor(pos).astype(jnp.int32), top_cell)
        frac = pos - low.astype(F32)
        high = low + 1
        low_chunk, low_lane = low >> 7, low & (LANES - 1)
        high_chunk, high_lane = high >> 7, high & (LANES - 1)
        relax = rr[:, part] / (1.0 + rr[:, part])
        marks[u, t, 0:SUB, :] = low_lane.astype(F32)
        marks[u, t, SUB : 2 * SUB, :] = low_chunk.astype(F32)
        for c in range(comps):
            at_low = at_high = None
            for h in range(chunks):
                row = gas_rows[c * chunks + h]
                got_low = jnp.take_along_axis(
                    row, low_lane, 1, mode="promise_in_bounds"
                )
                got_high = jnp.take_along_axis(
                    row, high_lane, 1, mode="promise_in_bounds"
                )
                at_low = got_low if h == 0 else jnp.where(low_chunk == h, got_low, at_low)
                at_high = (
                    got_high if h == 0 else jnp.where(high_chunk == h, got_high, at_high)
                )
            gas_at = at_low * (1.0 - frac) + at_high * frac
            vel = vv[c][:, part]
            updated = vel + relax * (gas_at - vel)
            store(c, part, updated)
            momentum = mm[:, part] * (vel - updated)
            for w, share in enumerate((momentum * (1.0 - frac), momentum * frac)):
                coarse = share.astype(BF16).astype(F32)
                row = (w * comps + c) * SUB
                shares[u, t, row : row + SUB, :] = coarse
                row += SUB * SUB
                shares[u, t, row : row + SUB, :] = share - coarse


def stage_two(space, acc, u, local, tiles):
    _, _, shares, marks, _, chunks = space
    pack = 2 * SUB
    place = lax.broadcasted_iota(jnp.int32, (pack, LANES), 0).astype(F32).astype(BF16)
    one, none = BF16(1.0), BF16(0.0)
    for b in range(SUB):
        spots, parts = [], []
        for t in range(tiles):
            share = shares[u, t, pl.ds(b, pack, stride=SUB), :].astype(BF16)
            lane = jnp.broadcast_to(marks[u, t, pl.ds(b, 1), :], (pack, LANES))
            chunk = jnp.broadcast_to(marks[u, t, pl.ds(SUB + b, 1), :], (pack, LANES))
            offset = lane.astype(BF16) - place
            chunk = chunk.astype(BF16)
            parts.append(
                jnp.concatenate(
                    [
                        jnp.where(chunk == BF16(h), share, none)
                        for h in range(chunks)
                    ],
                    0,
                )
            )
            spots.append(
                jnp.concatenate(
                    [
                        jnp.where(offset == BF16(pack * i), one, none)
                        for i in range(LANES // pack)
                    ],
                    0,
                )
            )
        both = lax.dot_general(
            jnp.concatenate(parts, 1),
            jnp.concatenate(spots, 1),
            (((1,), (1,)), ((), ())),
            preferred_element_type=F32,
        )
        for h in range(chunks):
            at = pl.ds(pl.multiple_of((local[b] * chunks + h) * SUB, SUB), SUB)
            row = h * pack
            acc[at, :] = acc[at, :] + (
                both[row : row + SUB] + both[row + SUB : row + pack]
            )


def mixed(center, x_next, x_last, y_next, y_last):
    chunks = len(center)
    lane = lax.broadcasted_iota(jnp.int32, center[0].shape, 1)
    ups = [pltpu.roll(value, LANES - 1, 1) for value in center] + [0.0]
    downs = [0.0] + [pltpu.roll(value, 1, 1) for value in center]
    result = []
    for h in range(chunks):
        above = jnp.where(lane == LANES - 1, ups[h + 1], ups[h])
        below = jnp.where(lane == 0, downs[h], downs[h + 1])
        around = ((x_next[h] + x_last[h]) + (y_next[h] + y_last[h])) + (above + below)
        result.append(center[h] * (1.0 - 6.0 * NU) + NU * around)
    return result


def stay_kernel(
    dims,
    columns,
    ext_in,
    x_low,
    x_high,
    y_low,
    y_high,
    corner_low,
    corner_high,
    state,
    keep,
    lines,
    acc,
    stayed,
    field,
    ext,
    mid,
    rows_scr,
    shares,
    marks,
):
    del ext_in
    _, _, cells_x, cells_y = dims
    comps, chunks = field.shape[:2]
    _, slots, width = state.shape
    top = SUB
    rows = pl.ds(top, cells_y)
    steps = rows_scr.shape[1]
    pitch = steps * SUB
    acc[...] = jnp.zeros_like(acc)

    planes = pl.ds(2, cells_x)
    for c in range(comps):
        for h in range(chunks):
            ext[c, h, 0:2, rows, :] = x_low[c, h]
            ext[c, h, 2 + cells_x : 4 + cells_x, rows, :] = x_high[c, h]
            ext[c, h, planes, top - 1, :] = y_low[c, h, 1]
            ext[c, h, planes, top + cells_y, :] = y_high[c, h, 0]
            for corner, y in ((corner_low, top - 1), (corner_high, top + cells_y)):
                for side, x in ((0, 1), (1, 2 + cells_x)):
                    line = corner[pl.ds((side * comps + c) * chunks + h, 1), :]
                    ext[c, h, x, pl.ds(y, 1), :] = line

    def plane(source, c, x):
        return mixed(
            *(
                [source[c, h, x + dx, pl.ds(top + dy, cells_y), :] for h in range(chunks)]
                for dx, dy in ((0, 0), (1, 0), (-1, 0), (0, 1), (0, -1))
            )
        )

    def first_plane(i, carry):
        for c in range(comps):
            for h, value in enumerate(plane(ext, c, 1 + i)):
                mid[c, h, i, rows, :] = value
        return carry

    lax.fori_loop(0, cells_x + 2, first_plane, 0)

    x_row = lax.broadcasted_iota(jnp.int32, (cells_x, LANES), 0)
    for c in range(comps):
        for face, near, far, inner, corner, row in (
            (y_low, 1, 0, top, corner_low, top - 1),
            (y_high, 0, 1, top + cells_y - 1, corner_high, top + cells_y),
        ):
            center = [face[c, h, near] for h in range(chunks)]
            left, right = [], []
            for h in range(chunks):
                first = corner[pl.ds(c * chunks + h, 1), :]
                last = corner[pl.ds((comps + c) * chunks + h, 1), :]
                left.append(jnp.where(x_row == 0, first, pltpu.roll(center[h], 1, 0)))
                right.append(
                    jnp.where(
                        x_row == cells_x - 1,
                        last,
                        pltpu.roll(center[h], cells_x - 1, 0),
                    )
                )
            outer = [face[c, h, far] for h in range(chunks)]
            inside = [ext[c, h, planes, inner, :] for h in range(chunks)]
            for h, value in enumerate(mixed(center, left, right, outer, inside)):
                mid[c, h, pl.ds(1, cells_x), row, :] = value

    def second_plane(i, carry):
        for c in range(comps):
            for h, value in enumerate(plane(mid, c, 1 + i)):
                field[c, h, i] = value
                at = i * cells_y * pitch + c * chunks + h
                lines[pl.ds(at, cells_y, stride=pitch), :] = value
        return carry

    lax.fori_loop(0, cells_x, second_plane, 0)

    space = (lines, rows_scr, shares, marks, comps, chunks)

    def staying(g, carry):
        locals_of = []
        for u in range(UNROLL):
            first = pl.multiple_of((g * UNROLL + u) * SUB, SUB)
            at = pl.ds(first, SUB)
            stays = jnp.tile(keep[at, :], (1, width // LANES)) > 0.0
            local = [local_of(columns[first + b], dims) for b in range(SUB)]
            locals_of.append(local)

            def store(c, part, value, at=at):
                stayed[c, at, part] = value

            stage_one(
                space,
                u,
                state[0, at, :],
                [jnp.where(stays, state[1 + c, at, :], 0.0) for c in range(3)],
                jnp.where(stays, state[4, at, :], 0.0),
                jnp.where(stays, state[5, at, :], 0.0),
                local,
                store,
            )
        for u in range(UNROLL):
            stage_two(space, acc, u, locals_of[u], width // LANES)
        return carry

    lax.fori_loop(0, slots // SUB // UNROLL, staying, 0)


def arrive_kernel(
    dims,
    capacity,
    in0,
    in1,
    in2,
    in3,
    lines,
    acc_in,
    stayed,
    field,
    gas_out,
    parcel_out,
    acc,
    gas_new,
    parcel_new,
    rows_scr,
    shares,
    marks,
    arrived,
    sems,
    plane_sems,
):
    del acc_in
    _, _, cells_x, cells_y = dims
    comps, chunks = field.shape[:2]
    _, slots, width = stayed.shape
    inboxes = (in0, in1, in2, in3)
    tails = [
        pltpu.make_async_copy(
            inboxes[d].at[pl.ds(FIELDS * capacity, SUB), pl.ds(0, LANES)],
            arrived.at[pl.ds(d * SUB, SUB), :],
            sems.at[d],
        )
        for d in range(4)
    ]
    for tail in tails:
        tail.start()
    kept = pltpu.make_async_copy(
        stayed, parcel_out.at[:, pl.ds(0, slots), :], sems.at[4]
    )
    kept.start()
    space = (lines, rows_scr, shares, marks, comps, chunks)
    for tail in tails:
        tail.wait()
    for d in range(4):
        inbox = inboxes[d]
        for start in range(0, capacity // SUB, UNROLL):
            groups = range(start, min(start + UNROLL, capacity // SUB))
            locals_of = []
            for u, g in enumerate(groups):
                first = g * SUB
                local = [
                    local_of(
                        arrived[d * SUB, d * capacity + first + b].astype(jnp.int32),
                        dims,
                    )
                    for b in range(SUB)
                ]
                locals_of.append(local)
                values = [
                    inbox[first + f * capacity : first + f * capacity + SUB, :]
                    for f in range(FIELDS)
                ]
                row = d * capacity + first

                def store(c, part, value, row=row):
                    parcel_new[c, row : row + SUB, part] = value

                stage_one(
                    space, u, values[0], values[1:4], values[4], values[5], local, store
                )
            for u, _ in enumerate(groups):
                stage_two(space, acc, u, locals_of[u], width // LANES)
    fresh = pltpu.make_async_copy(
        parcel_new, parcel_out.at[:, pl.ds(slots, 4 * capacity), :], sems.at[5]
    )
    fresh.start()

    lane_row = lax.broadcasted_iota(jnp.int32, (cells_y, LANES), 1)
    pitch = chunks * SUB

    def finish(i, carry):
        for c in range(comps):
            before = jnp.zeros((cells_y, LANES), F32)
            for h in range(chunks):
                base = i * cells_y * pitch + h * SUB + c
                low = acc[pl.ds(base, cells_y, stride=pitch), :]
                high = acc[pl.ds(base + comps, cells_y, stride=pitch), :]
                turned = pltpu.roll(high, 1, 1)
                moved = jnp.where(lane_row == 0, before, turned)
                before = turned
                gas_new[c, i, :, h * LANES : (h + 1) * LANES] = (
                    field[c, h, i] + low
                ) + moved
        pltpu.make_async_copy(
            gas_new.at[:, i], gas_out.at[:, i], plane_sems.at[i]
        ).start()
        return carry

    lax.fori_loop(0, cells_x, finish, 0)

    def settle(i, carry):
        pltpu.make_async_copy(
            gas_new.at[:, i], gas_out.at[:, i], plane_sems.at[i]
        ).wait()
        return carry

    lax.fori_loop(0, cells_x, settle, 0)
    kept.wait()
    fresh.wait()


def neighbour(value, axis, steps):
    count = lax.axis_size(axis)
    pairs = [(source, (source + steps) % count) for source in range(count)]
    return lax.ppermute(value, axis, pairs)


def params(mib):
    return pltpu.CompilerParams(vmem_limit_bytes=mib << 20)


def step(gas_velocity, parcel_z, parcel_velocity, parcel_rate, parcel_mass, parcel_column):
    comps, cells_x, cells_y, depth = gas_velocity.shape
    slots, width = parcel_z.shape
    capacity = slots // 4
    chunks = depth // LANES
    tiles = width // LANES
    cells = cells_x * cells_y
    x_count = lax.axis_size("gx")
    y_count = lax.axis_size(Y_AXES)
    dims = (x_count, y_count, cells_x, cells_y)
    velocity = jnp.transpose(parcel_velocity, (1, 0, 2))
    struct = lambda *shape: jax.ShapeDtypeStruct(shape, F32)

    ext_shape = (comps, chunks, cells_x + 4, cells_y + 2 * SUB, LANES)
    x_up, x_down, y_up, y_down, ext, state = pl.pallas_call(
        faces_kernel,
        out_shape=(
            struct(comps, chunks, 2, cells_y, LANES),
            struct(comps, chunks, 2, cells_y, LANES),
            struct(comps, chunks, 2, cells_x, LANES),
            struct(comps, chunks, 2, cells_x, LANES),
            struct(*ext_shape),
            struct(FIELDS, slots, width),
        ),
        in_specs=[HBM] * 5,
        out_specs=(VMEM,) * 6,
        scratch_shapes=[pltpu.SemaphoreType.DMA((chunks + 4,))],
        compiler_params=params(8),
        name="faces",
    )(gas_velocity, parcel_z, velocity, parcel_rate, parcel_mass)
    x_low = neighbour(x_up, "gx", 1)
    x_high = neighbour(x_down, "gx", -1)
    y_low = neighbour(y_up, Y_AXES, 1)
    y_high = neighbour(y_down, Y_AXES, -1)

    box = struct(FIELDS * capacity + SUB, width)
    outbox = pl.pallas_call(
        functools.partial(pack_kernel, dims, capacity),
        out_shape=(box,) * 4 + (struct(slots, LANES),),
        in_specs=[VMEM] * 2,
        out_specs=(VMEM,) * 5,
        compiler_params=params(8),
        name="pack",
    )(parcel_column.reshape(1, slots), state)
    in0 = neighbour(outbox[0], "gx", 1)
    in1 = neighbour(outbox[1], "gx", -1)

    line = struct(-(-2 * comps * chunks // SUB) * SUB, LANES)
    up, down, box2, box3 = pl.pallas_call(
        relay_kernel,
        out_shape=(line, line, box, box),
        in_specs=[VMEM] * 4,
        out_specs=(VMEM,) * 4,
        input_output_aliases={2: 2, 3: 3},
        compiler_params=params(8),
        name="relay",
    )(x_low, x_high, outbox[2], outbox[3])
    corner_low = neighbour(up, Y_AXES, 1)
    corner_high = neighbour(down, Y_AXES, -1)
    in2 = neighbour(box2, Y_AXES, 1)
    in3 = neighbour(box3, Y_AXES, -1)

    steps = -(-comps * chunks // SUB)
    scratch = [
        pltpu.VMEM((UNROLL, steps, SUB * SUB, LANES), F32),
        pltpu.VMEM((UNROLL, tiles, 2 * SUB * SUB, LANES), F32),
        pltpu.VMEM((UNROLL, tiles, 2 * SUB, LANES), F32),
    ]
    lines, acc, stayed, field, _ = pl.pallas_call(
        functools.partial(stay_kernel, dims),
        out_shape=(
            struct(cells * steps * SUB, LANES),
            struct(cells * chunks * SUB, LANES),
            struct(3, slots, width),
            struct(comps, chunks, cells_x, cells_y, LANES),
            struct(*ext_shape),
        ),
        in_specs=[SMEM] + [VMEM] * 9,
        out_specs=(VMEM,) * 5,
        scratch_shapes=[
            pltpu.VMEM((comps, chunks, cells_x + 2, cells_y + 2 * SUB, LANES), F32),
        ]
        + scratch,
        input_output_aliases={1: 4},
        compiler_params=params(16),
        name="stay",
    )(
        parcel_column,
        ext,
        x_low,
        x_high,
        y_low,
        y_high,
        corner_low,
        corner_high,
        state,
        outbox[4],
    )
    gas_out, updated, _ = pl.pallas_call(
        functools.partial(arrive_kernel, dims, capacity),
        out_shape=(
            struct(comps, cells_x, cells_y, depth),
            struct(3, slots + 4 * capacity, width),
            struct(cells * chunks * SUB, LANES),
        ),
        in_specs=[VMEM] * 8,
        out_specs=(HBM, HBM, VMEM),
        scratch_shapes=[
            pltpu.VMEM((comps, cells_x, cells_y, depth), F32),
            pltpu.VMEM((3, 4 * capacity, width), F32),
        ]
        + scratch
        + [
            pltpu.SMEM((4 * SUB, LANES), F32),
            pltpu.SemaphoreType.DMA((6,)),
            pltpu.SemaphoreType.DMA((cells_x,)),
        ],
        input_output_aliases={5: 2},
        compiler_params=params(16),
        name="arrive",
    )(in0, in1, in2, in3, lines, acc, stayed, field)
    return gas_out, jnp.transpose(updated, (1, 0, 2))


def solution(mesh):
    placed = (
        P(None, "gx", Y_AXES, None),
        P(("grp", "gx", "gy"), None),
        P(("grp", "gx", "gy"), None, None),
        P(("grp", "gx", "gy"), None),
        P(("grp", "gx", "gy"), None),
        P(("grp", "gx", "gy")),
    )
    return jax.shard_map(
        step,
        mesh=mesh,
        in_specs=placed,
        out_specs=(P(None, "gx", Y_AXES, None), P(("grp", "gx", "gy"), None, None)),
        check_vma=False,
    )
```

```python
import functools

import jax
import jax.numpy as jnp
from jax import lax
from jax.experimental import pallas as pl
from jax.experimental.pallas import tpu as pltpu
from jax.sharding import PartitionSpec as P


NU = 0.1
LANES = 128
SUB = 8
UNROLL = 2
FIELDS = 6
Y_AXES = ("grp", "gy")
F32 = jnp.float32
BF16 = jnp.bfloat16

VMEM = pl.BlockSpec(memory_space=pltpu.VMEM)
SMEM = pl.BlockSpec(memory_space=pltpu.SMEM)
HBM = pl.BlockSpec(memory_space=pltpu.HBM)


def quotient(value, by):
    if by & (by - 1) == 0:
        return value >> (by.bit_length() - 1)
    return lax.div(value, jnp.full_like(value, by))


def remainder(value, by):
    if by & (by - 1) == 0:
        return value & (by - 1)
    return lax.rem(value, jnp.full_like(value, by))


def y_place():
    return lax.axis_index("grp") * lax.axis_size("gy") + lax.axis_index("gy")


def heading_of(column, dims):
    x_count, y_count, cells_x, cells_y = dims
    rows_total = cells_y * y_count
    x_index, y_index = lax.axis_index("gx"), y_place()
    target_x = quotient(column, rows_total * cells_x)
    target_y = quotient(remainder(column, rows_total), cells_y)
    x_up, x_down = lax.rem(x_index + 1, x_count), lax.rem(x_index + x_count - 1, x_count)
    y_up, y_down = lax.rem(y_index + 1, y_count), lax.rem(y_index + y_count - 1, y_count)
    return jnp.where(
        target_x == x_up,
        1,
        jnp.where(
            target_x == x_down,
            2,
            jnp.where(target_y == y_up, 3, jnp.where(target_y == y_down, 4, 0)),
        ),
    )


def local_of(column, dims):
    _, y_count, cells_x, cells_y = dims
    x = remainder(quotient(column, cells_y * y_count), cells_x)
    return x * cells_y + remainder(column, cells_y)


def faces_kernel(
    gas, z, v, rate, mass, columns, x_up, x_down, y_up, y_down, ext, state, numbers, sems
):
    comps, cells_x, cells_y, depth = gas.shape
    chunks = depth // LANES
    copies = [
        pltpu.make_async_copy(
            gas.at[:, :, :, pl.ds(h * LANES, LANES)],
            ext.at[:, h, pl.ds(2, cells_x), pl.ds(SUB, cells_y), :],
            sems.at[h],
        )
        for h in range(chunks)
    ]
    for i, (source, target) in enumerate(
        (
            (z, state.at[0]),
            (v, state.at[pl.ds(1, 3)]),
            (rate, state.at[4]),
            (mass, state.at[5]),
            (columns, numbers),
        )
    ):
        copies.append(pltpu.make_async_copy(source, target, sems.at[chunks + i]))
    for copy in copies:
        copy.start()
    rows = pl.ds(SUB, cells_y)
    for h in range(chunks):
        copies[h].wait()
        for c in range(comps):
            for near in range(2):
                x_up[c, h, near] = ext[c, h, cells_x + near, rows, :]
                x_down[c, h, near] = ext[c, h, 2 + near, rows, :]
                planes = pl.ds(2, cells_x)
                y_up[c, h, near] = ext[c, h, planes, SUB + cells_y - 2 + near, :]
                y_down[c, h, near] = ext[c, h, planes, SUB + near, :]
    for copy in copies[chunks:]:
        copy.wait()


def selected(select, whole):
    first = whole.astype(BF16)
    rest = whole - first.astype(F32)
    second = rest.astype(BF16)
    third = (rest - second.astype(F32)).astype(BF16)
    return (
        jnp.dot(select, first, preferred_element_type=F32)
        + jnp.dot(select, second, preferred_element_type=F32)
    ) + jnp.dot(select, third, preferred_element_type=F32)


def numbers_at(values, select):
    slots = values.shape[1]
    digit = lax.broadcasted_iota(jnp.int32, (SUB, slots), 0)
    digits = jnp.where(
        digit == 0,
        values & 255,
        jnp.where(digit == 1, (values >> 8) & 255, jnp.where(digit == 2, values >> 16, 0)),
    )
    found = lax.dot_general(
        digits.astype(F32).astype(BF16),
        select,
        (((1,), (1,)), ((), ())),
        preferred_element_type=F32,
    )
    return found[0:1] + 256.0 * found[1:2] + 65536.0 * found[2:3]


def pack_kernel(dims, capacity, columns, state, box0, box1, box2, box3, keep, late):
    boxes = (box0, box1, box2, box3)
    _, slots, _ = state.shape
    _, _, cells_x, cells_y = dims
    column = columns[...]
    head = heading_of(column, dims)
    local = local_of(column, dims)
    x, y = quotient(local, cells_y), remainder(local, cells_y)
    waits = (head == 0) & ((x == 0) | (x == cells_x - 1))
    waits = waits & ((y == 0) | (y == cells_y - 1))
    head = jnp.where(waits, 5, head)
    code = lax.broadcasted_iota(jnp.int32, (SUB, slots), 0) + 1
    leaves = jnp.where(code == head, 1.0, 0.0)
    before = jnp.where(
        lax.broadcasted_iota(jnp.int32, (slots, slots), 0)
        < lax.broadcasted_iota(jnp.int32, (slots, slots), 1),
        1.0,
        0.0,
    )
    ranks = jnp.dot(
        leaves.astype(BF16), before.astype(BF16), preferred_element_type=F32
    )
    rank = jnp.sum(ranks * leaves, 0, keepdims=True).astype(jnp.int32)
    target = jnp.where(
        (head > 0) & (head < 5) & (rank < capacity), (head - 1) * capacity + rank, -1
    )
    select = jnp.where(
        lax.broadcasted_iota(jnp.int32, (4 * capacity, slots), 0) == target, 1.0, 0.0
    ).astype(BF16)
    late[...] = jnp.where(head == 5, rank, -1)
    for f in range(FIELDS):
        whole = state[f]
        moved = selected(select, whole)
        for d in range(4):
            boxes[d][f * capacity : (f + 1) * capacity, :] = moved[
                d * capacity : (d + 1) * capacity
            ]
    same = lax.broadcasted_iota(jnp.int32, (slots, slots), 0)
    same = same == lax.broadcasted_iota(jnp.int32, (slots, slots), 1)
    keep[...] = jnp.dot(
        jnp.where(same & (head == 0), 1.0, 0.0).astype(BF16),
        jnp.ones((slots, LANES), BF16),
        preferred_element_type=F32,
    )
    tail = numbers_at(column, select)
    for d in range(4):
        boxes[d][FIELDS * capacity : FIELDS * capacity + 1, 0 : 4 * capacity] = tail


def late_kernel(columns, late, state, box, info, acc):
    _, slots, _ = state.shape
    target = late[...]
    count = jnp.max(target) + 1
    rank = lax.broadcasted_iota(jnp.int32, (slots, slots), 0)
    select = jnp.where(rank == target, 1.0, 0.0).astype(BF16)
    info[0:1, 0:slots] = numbers_at(columns[...], select)
    slot = lax.broadcasted_iota(jnp.int32, (1, slots), 1)
    info[1:2, 0:slots] = numbers_at(slot, select)
    info[2:3, :] = jnp.full((1, info.shape[1]), count, jnp.int32).astype(F32)

    def fill(first, last):
        for f in range(FIELDS):
            box[f * slots + first : f * slots + last, :] = selected(
                select[first:last], state[f]
            )

    @pl.when(count > 0)
    def _():
        fill(0, 2 * SUB)

    @pl.when(count > 2 * SUB)
    def _():
        fill(2 * SUB, slots)

    acc[...] = jnp.zeros_like(acc)


def line_at(side, c, h, comps, chunks, capacity):
    line = (side * comps + c) * chunks + h
    row = FIELDS * capacity + 1 + line // 2
    lane = line % 2 * LANES
    return slice(row, row + 1), slice(lane, lane + LANES)


def relay_kernel(capacity, y_low, y_high, box0, box1, acc_in, out0, out1, acc):
    del box0, box1, acc_in, acc
    comps, chunks, _, cells_x, _ = y_low.shape
    for side, (face, near) in enumerate(((y_low, 1), (y_high, 0))):
        for c in range(comps):
            for h in range(chunks):
                rows, lanes = line_at(side, c, h, comps, chunks, capacity)
                out0[rows, lanes] = face[c, h, near, cells_x - 1 : cells_x, :]
                out1[rows, lanes] = face[c, h, near, 0:1, :]


def stage_one(space, u, zz, vv, rr, mm, local, store):
    lines, rows_scr, shares, marks, comps, chunks = space
    steps = rows_scr.shape[1]
    for b in range(SUB):
        for k in range(steps):
            at = pl.multiple_of((local[b] * steps + k) * SUB, SUB)
            rows_scr[u, k, b * SUB : (b + 1) * SUB, :] = lines[pl.ds(at, SUB), :]
    gas_rows = [
        rows_scr[u, r // SUB, pl.ds(r % SUB, SUB, stride=SUB), :]
        for r in range(comps * chunks)
    ]
    top_cell = chunks * LANES - 2
    for t in range(zz.shape[1] // LANES):
        part = slice(t * LANES, (t + 1) * LANES)
        pos = zz[:, part]
        low = jnp.minimum(jnp.floor(pos).astype(jnp.int32), top_cell)
        frac = pos - low.astype(F32)
        high = low + 1
        low_chunk, low_lane = low >> 7, low & (LANES - 1)
        high_chunk, high_lane = high >> 7, high & (LANES - 1)
        relax = rr[:, part] / (1.0 + rr[:, part])
        marks[u, t, 0:SUB, :] = low_lane.astype(F32)
        marks[u, t, SUB : 2 * SUB, :] = low_chunk.astype(F32)
        for c in range(comps):
            at_low = at_high = None
            for h in range(chunks):
                row = gas_rows[c * chunks + h]
                got_low = jnp.take_along_axis(
                    row, low_lane, 1, mode="promise_in_bounds"
                )
                got_high = jnp.take_along_axis(
                    row, high_lane, 1, mode="promise_in_bounds"
                )
                at_low = got_low if h == 0 else jnp.where(low_chunk == h, got_low, at_low)
                at_high = (
                    got_high if h == 0 else jnp.where(high_chunk == h, got_high, at_high)
                )
            gas_at = at_low * (1.0 - frac) + at_high * frac
            vel = vv[c][:, part]
            updated = vel + relax * (gas_at - vel)
            store(c, part, updated)
            momentum = mm[:, part] * (vel - updated)
            for w, share in enumerate((momentum * (1.0 - frac), momentum * frac)):
                coarse = share.astype(BF16).astype(F32)
                row = (w * comps + c) * SUB
                shares[u, t, row : row + SUB, :] = coarse
                row += SUB * SUB
                shares[u, t, row : row + SUB, :] = share - coarse


def stage_two(space, acc, u, local, tiles):
    _, _, shares, marks, _, chunks = space
    pack = 2 * SUB
    place = lax.broadcasted_iota(jnp.int32, (pack, LANES), 0).astype(F32).astype(BF16)
    one, none = BF16(1.0), BF16(0.0)
    for b in range(SUB):
        spots, parts = [], []
        for t in range(tiles):
            share = shares[u, t, pl.ds(b, pack, stride=SUB), :].astype(BF16)
            lane = jnp.broadcast_to(marks[u, t, pl.ds(b, 1), :], (pack, LANES))
            chunk = jnp.broadcast_to(marks[u, t, pl.ds(SUB + b, 1), :], (pack, LANES))
            offset = lane.astype(BF16) - place
            chunk = chunk.astype(BF16)
            parts.append(
                jnp.concatenate(
                    [
                        jnp.where(chunk == BF16(h), share, none)
                        for h in range(chunks)
                    ],
                    0,
                )
            )
            spots.append(
                jnp.concatenate(
                    [
                        jnp.where(offset == BF16(pack * i), one, none)
                        for i in range(LANES // pack)
                    ],
                    0,
                )
            )
        both = lax.dot_general(
            jnp.concatenate(parts, 1),
            jnp.concatenate(spots, 1),
            (((1,), (1,)), ((), ())),
            preferred_element_type=F32,
        )
        for h in range(chunks):
            at = pl.ds(pl.multiple_of((local[b] * chunks + h) * SUB, SUB), SUB)
            row = h * pack
            acc[at, :] = acc[at, :] + (
                both[row : row + SUB] + both[row + SUB : row + pack]
            )


def pipeline(space, acc, group, count, tiles):
    waiting = []
    for start in range(0, count + UNROLL, UNROLL):
        base = start // UNROLL % 2 * UNROLL
        fresh = []
        for u, g in enumerate(range(start, min(start + UNROLL, count))):
            taken = group(g)
            stage_one(space, base + u, *taken)
            fresh.append((base + u, taken[4]))
        for u, local in waiting:
            stage_two(space, acc, u, local, tiles)
        waiting = fresh


def mixed(center, x_next, x_last, y_next, y_last):
    chunks = len(center)
    lane = lax.broadcasted_iota(jnp.int32, center[0].shape, 1)
    ups = [pltpu.roll(value, LANES - 1, 1) for value in center] + [0.0]
    downs = [0.0] + [pltpu.roll(value, 1, 1) for value in center]
    result = []
    for h in range(chunks):
        above = jnp.where(lane == LANES - 1, ups[h + 1], ups[h])
        below = jnp.where(lane == 0, downs[h], downs[h + 1])
        around = ((x_next[h] + x_last[h]) + (y_next[h] + y_last[h])) + (above + below)
        result.append(center[h] * (1.0 - 6.0 * NU) + NU * around)
    return result


def stay_kernel(
    dims,
    columns,
    ext_in,
    acc_in,
    x_low,
    x_high,
    y_low,
    y_high,
    y_up,
    y_down,
    state,
    keep,
    lines,
    acc,
    stayed,
    field,
    ext,
    mid,
    rows_scr,
    shares,
    marks,
):
    del ext_in, acc_in
    _, _, cells_x, cells_y = dims
    comps, chunks = field.shape[:2]
    _, slots, width = state.shape
    top = SUB
    rows = pl.ds(top, cells_y)
    steps = rows_scr.shape[1]
    pitch = steps * SUB

    planes = pl.ds(2, cells_x)
    for c in range(comps):
        for h in range(chunks):
            ext[c, h, 0:2, rows, :] = x_low[c, h]
            ext[c, h, 2 + cells_x : 4 + cells_x, rows, :] = x_high[c, h]
            ext[c, h, planes, top - 1, :] = y_low[c, h, 1]
            ext[c, h, planes, top + cells_y, :] = y_high[c, h, 0]
            for x in (1, 2 + cells_x):
                for y in (top - 1, top + cells_y):
                    ext[c, h, x, y : y + 1, :] = jnp.zeros((1, LANES), F32)

    def plane(source, c, x):
        return mixed(
            *(
                [source[c, h, x + dx, pl.ds(top + dy, cells_y), :] for h in range(chunks)]
                for dx, dy in ((0, 0), (1, 0), (-1, 0), (0, 1), (0, -1))
            )
        )

    def first_plane(i, carry):
        for c in range(comps):
            for h, value in enumerate(plane(ext, c, 1 + i)):
                mid[c, h, i, rows, :] = value
        return carry

    lax.fori_loop(0, cells_x + 2, first_plane, 0, unroll=2)

    x_row = lax.broadcasted_iota(jnp.int32, (cells_x, LANES), 0)
    for c in range(comps):
        for side, face, near, far, own, row in (
            (0, y_low, 1, 0, y_down, top - 1),
            (1, y_high, 0, 1, y_up, top + cells_y),
        ):
            center = [face[c, h, near] for h in range(chunks)]
            left, right = [], []
            for h in range(chunks):
                left.append(jnp.where(x_row == 0, 0.0, pltpu.roll(center[h], 1, 0)))
                right.append(
                    jnp.where(
                        x_row == cells_x - 1, 0.0, pltpu.roll(center[h], cells_x - 1, 0)
                    )
                )
            outer = [face[c, h, far] for h in range(chunks)]
            inside = [own[c, h, side] for h in range(chunks)]
            for h, value in enumerate(mixed(center, left, right, outer, inside)):
                mid[c, h, pl.ds(1, cells_x), row, :] = value

    def second_plane(i, carry):
        for c in range(comps):
            for h, value in enumerate(plane(mid, c, 1 + i)):
                field[c, h, i] = value
                at = i * cells_y * pitch + c * chunks + h
                lines[pl.ds(at, cells_y, stride=pitch), :] = value
        return carry

    lax.fori_loop(0, cells_x, second_plane, 0, unroll=2)

    def staying(g):
        at = pl.ds(g * SUB, SUB)
        stays = jnp.tile(keep[at, :], (1, width // LANES)) > 0.0

        def store(c, part, value):
            stayed[c, at, part] = value

        return (
            state[0, at, :],
            [jnp.where(stays, state[1 + c, at, :], 0.0) for c in range(3)],
            jnp.where(stays, state[4, at, :], 0.0),
            jnp.where(stays, state[5, at, :], 0.0),
            [local_of(columns[g * SUB + b], dims) for b in range(SUB)],
            store,
        )

    space = (lines, rows_scr, shares, marks, comps, chunks)
    pipeline(space, acc, staying, slots // SUB, width // LANES)


def arrive_kernel(
    dims,
    capacity,
    in0,
    in1,
    in2,
    in3,
    late,
    info,
    lines_in,
    acc_in,
    stayed_in,
    field_in,
    gas_out,
    parcel_out,
    acc,
    lines,
    stayed,
    field,
    gas_new,
    parcel_new,
    rows_scr,
    shares,
    marks,
    arrived,
    late_info,
    one_group,
    sems,
    plane_sems,
):
    del lines_in, acc_in, stayed_in, field_in
    _, _, cells_x, cells_y = dims
    comps, chunks = field.shape[:2]
    slots, width = stayed.shape[1] - SUB, stayed.shape[2]
    inboxes = (in0, in1, in2, in3)
    tails = [
        pltpu.make_async_copy(
            inboxes[d].at[pl.ds(FIELDS * capacity, SUB), pl.ds(0, LANES)],
            arrived.at[pl.ds(d * SUB, SUB), :],
            sems.at[d],
        )
        for d in range(4)
    ]
    for tail in tails:
        tail.start()
    listed = pltpu.make_async_copy(info, late_info, sems.at[4])
    listed.start()

    for inbox, x in ((in0, 0), (in1, cells_x - 1)):
        for side, y in ((0, 0), (1, cells_y - 1)):
            for c in range(comps):
                for h in range(chunks):
                    rows, lanes = line_at(side, c, h, comps, chunks, capacity)
                    part = (2.0 * NU * NU) * inbox[rows, lanes]
                    whole = field[c, h, x, y : y + 1, :] + part
                    field[c, h, x, y : y + 1, :] = whole
                    row = (x * cells_y + y) * rows_scr.shape[1] * SUB + c * chunks + h
                    lines[row : row + 1, :] = whole

    space = (lines, rows_scr, shares, marks, comps, chunks)
    listed.wait()
    count = late_info[2, 0].astype(jnp.int32)

    def waited(g, carry):
        first = pl.multiple_of(g * SUB, SUB)
        local = [
            local_of(late_info[0, first + b].astype(jnp.int32), dims)
            for b in range(SUB)
        ]

        def store(c, part, value):
            one_group[c, :, part] = value

        values = [
            late[pl.ds(pl.multiple_of(first + f * slots, SUB), SUB), :]
            for f in range(FIELDS)
        ]
        stage_one(space, 0, values[0], values[1:4], values[4], values[5], local, store)
        stage_two(space, acc, 0, local, width // LANES)
        for b in range(SUB):
            slot = jnp.where(
                first + b < count, late_info[1, first + b].astype(jnp.int32), slots
            )
            for c in range(3):
                stayed[c, pl.ds(slot, 1), :] = one_group[c, b : b + 1, :]
        return carry

    lax.fori_loop(0, (count + SUB - 1) >> 3, waited, 0)
    kept = pltpu.make_async_copy(
        stayed.at[:, pl.ds(0, slots), :], parcel_out.at[:, pl.ds(0, slots), :], sems.at[5]
    )
    kept.start()
    for tail in tails:
        tail.wait()
    per_box = capacity // SUB

    def arriving(g):
        d, first = g // per_box, g % per_box * SUB
        inbox, row = inboxes[d], g * SUB
        values = [
            inbox[first + f * capacity : first + f * capacity + SUB, :]
            for f in range(FIELDS)
        ]

        def store(c, part, value):
            parcel_new[c, row : row + SUB, part] = value

        local = [
            local_of(arrived[d * SUB, row + b].astype(jnp.int32), dims)
            for b in range(SUB)
        ]
        return values[0], values[1:4], values[4], values[5], local, store

    pipeline(space, acc, arriving, 4 * per_box, width // LANES)
    fresh = pltpu.make_async_copy(
        parcel_new, parcel_out.at[:, pl.ds(slots, 4 * capacity), :], sems.at[6]
    )
    fresh.start()

    lane_row = lax.broadcasted_iota(jnp.int32, (cells_y, LANES), 1)
    pitch = chunks * SUB

    def finish(i, carry):
        for c in range(comps):
            before = jnp.zeros((cells_y, LANES), F32)
            for h in range(chunks):
                base = i * cells_y * pitch + h * SUB + c
                low = acc[pl.ds(base, cells_y, stride=pitch), :]
                high = acc[pl.ds(base + comps, cells_y, stride=pitch), :]
                turned = pltpu.roll(high, 1, 1)
                moved = jnp.where(lane_row == 0, before, turned)
                before = turned
                gas_new[c, i, :, h * LANES : (h + 1) * LANES] = (
                    field[c, h, i] + low
                ) + moved
        pltpu.make_async_copy(
            gas_new.at[:, i], gas_out.at[:, i], plane_sems.at[i]
        ).start()
        return carry

    lax.fori_loop(0, cells_x, finish, 0, unroll=2)

    def settle(i, carry):
        pltpu.make_async_copy(
            gas_new.at[:, i], gas_out.at[:, i], plane_sems.at[i]
        ).wait()
        return carry

    lax.fori_loop(0, cells_x, settle, 0)
    kept.wait()
    fresh.wait()


def neighbour(value, axis, steps):
    count = lax.axis_size(axis)
    pairs = [(source, (source + steps) % count) for source in range(count)]
    return lax.ppermute(value, axis, pairs)


def params(mib):
    return pltpu.CompilerParams(vmem_limit_bytes=mib << 20)


def step(gas_velocity, parcel_z, parcel_velocity, parcel_rate, parcel_mass, parcel_column):
    comps, cells_x, cells_y, depth = gas_velocity.shape
    slots, width = parcel_z.shape
    capacity = slots // 4
    chunks = depth // LANES
    tiles = width // LANES
    cells = cells_x * cells_y
    x_count = lax.axis_size("gx")
    y_count = lax.axis_size(Y_AXES)
    dims = (x_count, y_count, cells_x, cells_y)
    velocity = jnp.transpose(parcel_velocity, (1, 0, 2))
    struct = lambda *shape: jax.ShapeDtypeStruct(shape, F32)

    ext_shape = (comps, chunks, cells_x + 4, cells_y + 2 * SUB, LANES)
    x_up, x_down, y_up, y_down, ext, state, numbers = pl.pallas_call(
        faces_kernel,
        out_shape=(
            struct(comps, chunks, 2, cells_y, LANES),
            struct(comps, chunks, 2, cells_y, LANES),
            struct(comps, chunks, 2, cells_x, LANES),
            struct(comps, chunks, 2, cells_x, LANES),
            struct(*ext_shape),
            struct(FIELDS, slots, width),
            jax.ShapeDtypeStruct((1, slots), jnp.int32),
        ),
        in_specs=[HBM] * 6,
        out_specs=(VMEM,) * 7,
        scratch_shapes=[pltpu.SemaphoreType.DMA((chunks + 5,))],
        compiler_params=params(8),
        name="faces",
    )(
        *(
            pltpu.with_memory_space_constraint(value, pltpu.HBM)
            for value in (
                gas_velocity,
                parcel_z,
                velocity,
                parcel_rate,
                parcel_mass,
                parcel_column.reshape(1, slots),
            )
        )
    )
    x_low = neighbour(x_up, "gx", 1)
    x_high = neighbour(x_down, "gx", -1)
    y_low = neighbour(y_up, Y_AXES, 1)
    y_high = neighbour(y_down, Y_AXES, -1)

    box = struct(FIELDS * capacity + SUB, width)
    lines_in_box = -(-(1 + comps * chunks) // SUB) * SUB
    long_box = struct(FIELDS * capacity + lines_in_box, width)
    outbox = pl.pallas_call(
        functools.partial(pack_kernel, dims, capacity),
        out_shape=(
            long_box,
            long_box,
            box,
            box,
            struct(slots, LANES),
            jax.ShapeDtypeStruct((1, slots), jnp.int32),
        ),
        in_specs=[VMEM] * 2,
        out_specs=(VMEM,) * 6,
        compiler_params=params(8),
        name="pack",
    )(numbers, state)
    in2 = neighbour(outbox[2], Y_AXES, 1)
    in3 = neighbour(outbox[3], Y_AXES, -1)

    acc_struct = struct(cells * chunks * SUB, LANES)
    late, info, acc = pl.pallas_call(
        late_kernel,
        out_shape=(
            struct(FIELDS * slots, width),
            struct(SUB, max(LANES, slots)),
            acc_struct,
        ),
        in_specs=[VMEM] * 3,
        out_specs=(VMEM,) * 3,
        compiler_params=params(8),
        name="late",
    )(numbers, outbox[5], state)
    box0, box1, acc = pl.pallas_call(
        functools.partial(relay_kernel, capacity),
        out_shape=(long_box, long_box, acc_struct),
        in_specs=[VMEM] * 5,
        out_specs=(VMEM,) * 3,
        input_output_aliases={2: 0, 3: 1, 4: 2},
        compiler_params=params(8),
        name="relay",
    )(y_low, y_high, outbox[0], outbox[1], acc)
    in0 = neighbour(box0, "gx", 1)
    in1 = neighbour(box1, "gx", -1)

    steps = -(-comps * chunks // SUB)
    scratch = [
        pltpu.VMEM((2 * UNROLL, steps, SUB * SUB, LANES), F32),
        pltpu.VMEM((2 * UNROLL, tiles, 2 * SUB * SUB, LANES), F32),
        pltpu.VMEM((2 * UNROLL, tiles, 2 * SUB, LANES), F32),
    ]
    lines, acc, stayed, field, _ = pl.pallas_call(
        functools.partial(stay_kernel, dims),
        out_shape=(
            struct(cells * steps * SUB, LANES),
            acc_struct,
            struct(3, slots + SUB, width),
            struct(comps, chunks, cells_x, cells_y, LANES),
            struct(*ext_shape),
        ),
        in_specs=[SMEM] + [VMEM] * 10,
        out_specs=(VMEM,) * 5,
        scratch_shapes=[
            pltpu.VMEM((comps, chunks, cells_x + 2, cells_y + 2 * SUB, LANES), F32),
        ]
        + scratch,
        input_output_aliases={1: 4, 2: 1},
        compiler_params=params(16),
        name="stay",
    )(
        parcel_column,
        ext,
        acc,
        x_low,
        x_high,
        y_low,
        y_high,
        y_up,
        y_down,
        state,
        outbox[4],
    )
    gas_out, updated = pl.pallas_call(
        functools.partial(arrive_kernel, dims, capacity),
        out_shape=(
            struct(comps, cells_x, cells_y, depth),
            struct(3, slots + 4 * capacity, width),
            acc_struct,
            struct(cells * steps * SUB, LANES),
            struct(3, slots + SUB, width),
            struct(comps, chunks, cells_x, cells_y, LANES),
        ),
        in_specs=[VMEM] * 10,
        out_specs=(HBM, HBM) + (VMEM,) * 4,
        scratch_shapes=[
            pltpu.VMEM((comps, cells_x, cells_y, depth), F32),
            pltpu.VMEM((3, 4 * capacity, width), F32),
        ]
        + scratch
        + [
            pltpu.SMEM((4 * SUB, LANES), F32),
            pltpu.SMEM((SUB, max(LANES, slots)), F32),
            pltpu.VMEM((3, SUB, width), F32),
            pltpu.SemaphoreType.DMA((7,)),
            pltpu.SemaphoreType.DMA((cells_x,)),
        ],
        input_output_aliases={6: 3, 7: 2, 8: 4, 9: 5},
        compiler_params=params(16),
        name="arrive",
    )(in0, in1, in2, in3, late, info, lines, acc, stayed, field)[:2]
    return gas_out, jnp.transpose(updated, (1, 0, 2))


def solution(mesh):
    placed = (
        P(None, "gx", Y_AXES, None),
        P(("grp", "gx", "gy"), None),
        P(("grp", "gx", "gy"), None, None),
        P(("grp", "gx", "gy"), None),
        P(("grp", "gx", "gy"), None),
        P(("grp", "gx", "gy")),
    )
    return jax.shard_map(
        step,
        mesh=mesh,
        in_specs=placed,
        out_specs=(P(None, "gx", Y_AXES, None), P(("grp", "gx", "gy"), None, None)),
        check_vma=False,
    )
```

```python
import functools

import jax
import jax.numpy as jnp
from jax import lax
from jax.experimental import pallas as pl
from jax.experimental.pallas import tpu as pltpu
from jax.sharding import PartitionSpec as P


NU = 0.1
LANES = 128
SUB = 8
SPAN = 64
UNROLL = 2
FIELDS = 6
Y_AXES = ("grp", "gy")
F32 = jnp.float32
BF16 = jnp.bfloat16

VMEM = pl.BlockSpec(memory_space=pltpu.VMEM)
SMEM = pl.BlockSpec(memory_space=pltpu.SMEM)
HBM = pl.BlockSpec(memory_space=pltpu.HBM)


def quotient(value, by):
    if by & (by - 1) == 0:
        return value >> (by.bit_length() - 1)
    return lax.div(value, jnp.full_like(value, by))


def remainder(value, by):
    if by & (by - 1) == 0:
        return value & (by - 1)
    return lax.rem(value, jnp.full_like(value, by))


def y_place():
    return lax.axis_index("grp") * lax.axis_size("gy") + lax.axis_index("gy")


def heading_of(column, dims):
    x_count, y_count, cells_x, cells_y = dims
    rows_total = cells_y * y_count
    x_index, y_index = lax.axis_index("gx"), y_place()
    target_x = quotient(column, rows_total * cells_x)
    target_y = quotient(remainder(column, rows_total), cells_y)
    x_up, x_down = lax.rem(x_index + 1, x_count), lax.rem(x_index + x_count - 1, x_count)
    y_up, y_down = lax.rem(y_index + 1, y_count), lax.rem(y_index + y_count - 1, y_count)
    return jnp.where(
        target_x == x_up,
        1,
        jnp.where(
            target_x == x_down,
            2,
            jnp.where(target_y == y_up, 3, jnp.where(target_y == y_down, 4, 0)),
        ),
    )


def local_of(column, dims):
    _, y_count, cells_x, cells_y = dims
    x = remainder(quotient(column, cells_y * y_count), cells_x)
    return x * cells_y + remainder(column, cells_y)


def faces_kernel(
    gas, z, v, rate, mass, columns, x_up, x_down, y_up, y_down, ext, state, numbers, sems
):
    comps, cells_x, cells_y, depth = gas.shape
    chunks = depth // LANES
    copies = [
        pltpu.make_async_copy(
            gas.at[:, :, :, pl.ds(h * LANES, LANES)],
            ext.at[:, h, pl.ds(2, cells_x), pl.ds(SUB, cells_y), :],
            sems.at[h],
        )
        for h in range(chunks)
    ]
    for i, (source, target) in enumerate(
        (
            (z, state.at[0]),
            (v, state.at[pl.ds(1, 3)]),
            (rate, state.at[4]),
            (mass, state.at[5]),
            (columns, numbers),
        )
    ):
        copies.append(pltpu.make_async_copy(source, target, sems.at[chunks + i]))
    for copy in copies:
        copy.start()
    rows = pl.ds(SUB, cells_y)
    for h in range(chunks):
        copies[h].wait()
        for c in range(comps):
            for near in range(2):
                x_up[c, h, near] = ext[c, h, cells_x + near, rows, :]
                x_down[c, h, near] = ext[c, h, 2 + near, rows, :]
                planes = pl.ds(2, cells_x)
                y_up[c, h, near] = ext[c, h, planes, SUB + cells_y - 2 + near, :]
                y_down[c, h, near] = ext[c, h, planes, SUB + near, :]
    for copy in copies[chunks:]:
        copy.wait()


def selected(select, whole):
    first = whole.astype(BF16)
    rest = whole - first.astype(F32)
    second = rest.astype(BF16)
    third = (rest - second.astype(F32)).astype(BF16)
    return (
        jnp.dot(select, first, preferred_element_type=F32)
        + jnp.dot(select, second, preferred_element_type=F32)
    ) + jnp.dot(select, third, preferred_element_type=F32)


def numbers_at(values, select):
    slots = values.shape[1]
    digit = lax.broadcasted_iota(jnp.int32, (SUB, slots), 0)
    digits = jnp.where(
        digit == 0,
        values & 255,
        jnp.where(digit == 1, (values >> 8) & 255, jnp.where(digit == 2, values >> 16, 0)),
    )
    found = lax.dot_general(
        digits.astype(F32).astype(BF16),
        select,
        (((1,), (1,)), ((), ())),
        preferred_element_type=F32,
    )
    return found[0:1] + 256.0 * found[1:2] + 65536.0 * found[2:3]


def pack_kernel(dims, capacity, columns, state, box0, box1, box2, box3, keep, late):
    boxes = (box0, box1, box2, box3)
    _, slots, _ = state.shape
    _, _, cells_x, cells_y = dims
    column = columns[...]
    head = heading_of(column, dims)
    local = local_of(column, dims)
    x, y = quotient(local, cells_y), remainder(local, cells_y)
    waits = (head == 0) & ((x == 0) | (x == cells_x - 1))
    waits = waits & ((y == 0) | (y == cells_y - 1))
    head = jnp.where(waits, 5, head)
    code = lax.broadcasted_iota(jnp.int32, (SUB, slots), 0) + 1
    leaves = jnp.where(code == head, 1.0, 0.0)
    before = jnp.where(
        lax.broadcasted_iota(jnp.int32, (slots, slots), 0)
        < lax.broadcasted_iota(jnp.int32, (slots, slots), 1),
        1.0,
        0.0,
    )
    ranks = jnp.dot(
        leaves.astype(BF16), before.astype(BF16), preferred_element_type=F32
    )
    rank = jnp.sum(ranks * leaves, 0, keepdims=True).astype(jnp.int32)
    target = jnp.where(
        (head > 0) & (head < 5) & (rank < capacity), (head - 1) * capacity + rank, -1
    )
    select = jnp.where(
        lax.broadcasted_iota(jnp.int32, (4 * capacity, slots), 0) == target, 1.0, 0.0
    ).astype(BF16)
    late[...] = jnp.where(head == 5, rank, -1)
    for f in range(FIELDS):
        whole = state[f]
        moved = selected(select, whole)
        for d in range(4):
            boxes[d][f * capacity : (f + 1) * capacity, :] = moved[
                d * capacity : (d + 1) * capacity
            ]
    same = lax.broadcasted_iota(jnp.int32, (slots, slots), 0)
    same = same == lax.broadcasted_iota(jnp.int32, (slots, slots), 1)
    keep[...] = jnp.dot(
        jnp.where(same & (head == 0), 1.0, 0.0).astype(BF16),
        jnp.ones((slots, LANES), BF16),
        preferred_element_type=F32,
    )
    tail = numbers_at(column, select)
    for d in range(4):
        boxes[d][FIELDS * capacity : FIELDS * capacity + 1, 0 : 4 * capacity] = tail


def late_kernel(columns, late, state, box, info, acc):
    _, slots, _ = state.shape
    target = late[...]
    count = jnp.max(target) + 1
    rank = lax.broadcasted_iota(jnp.int32, (slots, slots), 0)
    select = jnp.where(rank == target, 1.0, 0.0).astype(BF16)
    info[0:1, 0:slots] = numbers_at(columns[...], select)
    slot = lax.broadcasted_iota(jnp.int32, (1, slots), 1)
    info[1:2, 0:slots] = numbers_at(slot, select)
    info[2:3, :] = jnp.full((1, info.shape[1]), count, jnp.int32).astype(F32)

    def fill(first, last):
        for f in range(FIELDS):
            box[f * slots + first : f * slots + last, :] = selected(
                select[first:last], state[f]
            )

    @pl.when(count > 0)
    def _():
        fill(0, 2 * SUB)

    @pl.when(count > 2 * SUB)
    def _():
        fill(2 * SUB, slots)

    acc[...] = jnp.zeros_like(acc)


def line_at(side, c, h, comps, chunks, capacity):
    line = (side * comps + c) * chunks + h
    row = FIELDS * capacity + 1 + line // 2
    lane = line % 2 * LANES
    return slice(row, row + 1), slice(lane, lane + LANES)


def relay_kernel(capacity, y_low, y_high, box0, box1, acc_in, out0, out1, acc):
    del box0, box1, acc_in, acc
    comps, chunks, _, cells_x, _ = y_low.shape
    for side, (face, near) in enumerate(((y_low, 1), (y_high, 0))):
        for c in range(comps):
            for h in range(chunks):
                rows, lanes = line_at(side, c, h, comps, chunks, capacity)
                out0[rows, lanes] = face[c, h, near, cells_x - 1 : cells_x, :]
                out1[rows, lanes] = face[c, h, near, 0:1, :]


def stage_one(space, u, zz, vv, rr, mm, local, store):
    lines, rows_scr, shares, marks, comps, chunks = space
    steps = rows_scr.shape[1]
    for b in range(SUB):
        for k in range(steps):
            at = pl.multiple_of((local[b] * steps + k) * SUB, SUB)
            rows_scr[u, k, b * SUB : (b + 1) * SUB, :] = lines[pl.ds(at, SUB), :]
    gas_rows = [
        rows_scr[u, r // SUB, pl.ds(r % SUB, SUB, stride=SUB), :]
        for r in range(comps * chunks)
    ]
    top_cell = chunks * LANES - 2
    for t in range(zz.shape[1] // LANES):
        part = slice(t * LANES, (t + 1) * LANES)
        pos = zz[:, part]
        low = jnp.minimum(jnp.floor(pos).astype(jnp.int32), top_cell)
        frac = pos - low.astype(F32)
        high = low + 1
        low_chunk, low_lane = low >> 7, low & (LANES - 1)
        high_chunk, high_lane = high >> 7, high & (LANES - 1)
        relax = rr[:, part] / (1.0 + rr[:, part])
        marks[u, t, 0:SUB, :] = (low & (SPAN - 1)).astype(F32)
        marks[u, t, SUB : 2 * SUB, :] = (low >> (SPAN.bit_length() - 1)).astype(F32)
        for c in range(comps):
            at_low = at_high = None
            for h in range(chunks):
                row = gas_rows[c * chunks + h]
                got_low = jnp.take_along_axis(
                    row, low_lane, 1, mode="promise_in_bounds"
                )
                got_high = jnp.take_along_axis(
                    row, high_lane, 1, mode="promise_in_bounds"
                )
                at_low = got_low if h == 0 else jnp.where(low_chunk == h, got_low, at_low)
                at_high = (
                    got_high if h == 0 else jnp.where(high_chunk == h, got_high, at_high)
                )
            gas_at = at_low * (1.0 - frac) + at_high * frac
            vel = vv[c][:, part]
            updated = vel + relax * (gas_at - vel)
            store(c, part, updated)
            momentum = mm[:, part] * (vel - updated)
            for w, share in enumerate((momentum * (1.0 - frac), momentum * frac)):
                coarse = share.astype(BF16).astype(F32)
                row = (w * comps + c) * SUB
                shares[u, t, row : row + SUB, :] = coarse
                row += SUB * SUB
                shares[u, t, row : row + SUB, :] = share - coarse


def stage_two(space, acc, u, local, tiles):
    _, _, shares, marks, _, chunks = space
    pack = 2 * SUB
    per_chunk = LANES // SPAN
    place = lax.broadcasted_iota(jnp.int32, (pack, LANES), 0).astype(F32).astype(BF16)
    one, none = BF16(1.0), BF16(0.0)
    for b in range(SUB):
        spots, parts = [], []
        for t in range(tiles):
            share = shares[u, t, pl.ds(b, pack, stride=SUB), :].astype(BF16)
            lane = jnp.broadcast_to(marks[u, t, pl.ds(b, 1), :], (pack, LANES))
            span = jnp.broadcast_to(marks[u, t, pl.ds(SUB + b, 1), :], (pack, LANES))
            offset = lane.astype(BF16) - place
            span = span.astype(BF16)
            parts.append(
                jnp.concatenate(
                    [
                        jnp.where(span == BF16(q), share, none)
                        for q in range(chunks * per_chunk)
                    ],
                    0,
                )
            )
            spots.append(
                jnp.concatenate(
                    [
                        jnp.where(offset == BF16(pack * i), one, none)
                        for i in range(SPAN // pack)
                    ],
                    0,
                )
            )
        both = lax.dot_general(
            jnp.concatenate(parts, 1),
            jnp.concatenate(spots, 1),
            (((1,), (1,)), ((), ())),
            preferred_element_type=F32,
        )
        sums = [
            both[q * pack : q * pack + SUB] + both[q * pack + SUB : (q + 1) * pack]
            for q in range(chunks * per_chunk)
        ]
        for h in range(chunks):
            at = pl.ds(pl.multiple_of((local[b] * chunks + h) * SUB, SUB), SUB)
            acc[at, :] = acc[at, :] + jnp.concatenate(
                sums[h * per_chunk : (h + 1) * per_chunk], 1
            )


def pipeline(space, acc, group, count, tiles):
    waiting = []
    for start in range(0, count + UNROLL, UNROLL):
        base = start // UNROLL % 2 * UNROLL
        fresh = []
        for u, g in enumerate(range(start, min(start + UNROLL, count))):
            taken = group(g)
            stage_one(space, base + u, *taken)
            fresh.append((base + u, taken[4]))
        for u, local in waiting:
            stage_two(space, acc, u, local, tiles)
        waiting = fresh


def mixed(center, x_next, x_last, y_next, y_last):
    chunks = len(center)
    lane = lax.broadcasted_iota(jnp.int32, center[0].shape, 1)
    ups = [pltpu.roll(value, LANES - 1, 1) for value in center] + [0.0]
    downs = [0.0] + [pltpu.roll(value, 1, 1) for value in center]
    result = []
    for h in range(chunks):
        above = jnp.where(lane == LANES - 1, ups[h + 1], ups[h])
        below = jnp.where(lane == 0, downs[h], downs[h + 1])
        around = ((x_next[h] + x_last[h]) + (y_next[h] + y_last[h])) + (above + below)
        result.append(center[h] * (1.0 - 6.0 * NU) + NU * around)
    return result


def stay_kernel(
    dims,
    columns,
    ext_in,
    acc_in,
    x_low,
    x_high,
    y_low,
    y_high,
    y_up,
    y_down,
    state,
    keep,
    lines,
    acc,
    stayed,
    field,
    ext,
    mid,
    rows_scr,
    shares,
    marks,
):
    del ext_in, acc_in
    _, _, cells_x, cells_y = dims
    comps, chunks = field.shape[:2]
    _, slots, width = state.shape
    top = SUB
    rows = pl.ds(top, cells_y)
    steps = rows_scr.shape[1]
    pitch = steps * SUB

    planes = pl.ds(2, cells_x)
    for c in range(comps):
        for h in range(chunks):
            ext[c, h, 0:2, rows, :] = x_low[c, h]
            ext[c, h, 2 + cells_x : 4 + cells_x, rows, :] = x_high[c, h]
            ext[c, h, planes, top - 1, :] = y_low[c, h, 1]
            ext[c, h, planes, top + cells_y, :] = y_high[c, h, 0]
            for x in (1, 2 + cells_x):
                for y in (top - 1, top + cells_y):
                    ext[c, h, x, y : y + 1, :] = jnp.zeros((1, LANES), F32)

    def plane(source, c, x):
        return mixed(
            *(
                [source[c, h, x + dx, pl.ds(top + dy, cells_y), :] for h in range(chunks)]
                for dx, dy in ((0, 0), (1, 0), (-1, 0), (0, 1), (0, -1))
            )
        )

    def first_plane(i, carry):
        for c in range(comps):
            for h, value in enumerate(plane(ext, c, 1 + i)):
                mid[c, h, i, rows, :] = value
        return carry

    lax.fori_loop(0, cells_x + 2, first_plane, 0, unroll=(cells_x + 2) // 2)

    x_row = lax.broadcasted_iota(jnp.int32, (cells_x, LANES), 0)
    for c in range(comps):
        for side, face, near, far, own, row in (
            (0, y_low, 1, 0, y_down, top - 1),
            (1, y_high, 0, 1, y_up, top + cells_y),
        ):
            center = [face[c, h, near] for h in range(chunks)]
            left, right = [], []
            for h in range(chunks):
                left.append(jnp.where(x_row == 0, 0.0, pltpu.roll(center[h], 1, 0)))
                right.append(
                    jnp.where(
                        x_row == cells_x - 1, 0.0, pltpu.roll(center[h], cells_x - 1, 0)
                    )
                )
            outer = [face[c, h, far] for h in range(chunks)]
            inside = [own[c, h, side] for h in range(chunks)]
            for h, value in enumerate(mixed(center, left, right, outer, inside)):
                mid[c, h, pl.ds(1, cells_x), row, :] = value

    def second_plane(i, carry):
        for c in range(comps):
            for h, value in enumerate(plane(mid, c, 1 + i)):
                field[c, h, i] = value
                at = i * cells_y * pitch + c * chunks + h
                lines[pl.ds(at, cells_y, stride=pitch), :] = value
        return carry

    lax.fori_loop(0, cells_x, second_plane, 0, unroll=True)

    def staying(g):
        at = pl.ds(g * SUB, SUB)
        stays = jnp.tile(keep[at, :], (1, width // LANES)) > 0.0

        def store(c, part, value):
            stayed[c, at, part] = value

        return (
            state[0, at, :],
            [jnp.where(stays, state[1 + c, at, :], 0.0) for c in range(3)],
            jnp.where(stays, state[4, at, :], 0.0),
            jnp.where(stays, state[5, at, :], 0.0),
            [local_of(columns[g * SUB + b], dims) for b in range(SUB)],
            store,
        )

    space = (lines, rows_scr, shares, marks, comps, chunks)
    pipeline(space, acc, staying, slots // SUB, width // LANES)


def arrive_kernel(
    dims,
    capacity,
    in0,
    in1,
    in2,
    in3,
    late,
    info,
    lines_in,
    acc_in,
    stayed_in,
    field_in,
    gas_out,
    parcel_out,
    acc,
    lines,
    stayed,
    field,
    gas_new,
    parcel_new,
    rows_scr,
    shares,
    marks,
    arrived,
    late_info,
    one_group,
    sems,
    plane_sems,
):
    del lines_in, acc_in, stayed_in, field_in
    _, _, cells_x, cells_y = dims
    comps, chunks = field.shape[:2]
    slots, width = stayed.shape[1] - SUB, stayed.shape[2]
    inboxes = (in0, in1, in2, in3)
    tails = [
        pltpu.make_async_copy(
            inboxes[d].at[pl.ds(FIELDS * capacity, SUB), pl.ds(0, LANES)],
            arrived.at[pl.ds(d * SUB, SUB), :],
            sems.at[d],
        )
        for d in range(4)
    ]
    for tail in tails:
        tail.start()
    listed = pltpu.make_async_copy(info, late_info, sems.at[4])
    listed.start()

    for inbox, x in ((in0, 0), (in1, cells_x - 1)):
        for side, y in ((0, 0), (1, cells_y - 1)):
            for c in range(comps):
                for h in range(chunks):
                    rows, lanes = line_at(side, c, h, comps, chunks, capacity)
                    part = (2.0 * NU * NU) * inbox[rows, lanes]
                    whole = field[c, h, x, y : y + 1, :] + part
                    field[c, h, x, y : y + 1, :] = whole
                    row = (x * cells_y + y) * rows_scr.shape[1] * SUB + c * chunks + h
                    lines[row : row + 1, :] = whole

    space = (lines, rows_scr, shares, marks, comps, chunks)
    listed.wait()
    count = late_info[2, 0].astype(jnp.int32)

    def waited(g, carry):
        first = pl.multiple_of(g * SUB, SUB)
        local = [
            local_of(late_info[0, first + b].astype(jnp.int32), dims)
            for b in range(SUB)
        ]

        def store(c, part, value):
            one_group[c, :, part] = value

        values = [
            late[pl.ds(pl.multiple_of(first + f * slots, SUB), SUB), :]
            for f in range(FIELDS)
        ]
        stage_one(space, 0, values[0], values[1:4], values[4], values[5], local, store)
        stage_two(space, acc, 0, local, width // LANES)
        for b in range(SUB):
            slot = jnp.where(
                first + b < count, late_info[1, first + b].astype(jnp.int32), slots
            )
            for c in range(3):
                stayed[c, pl.ds(slot, 1), :] = one_group[c, b : b + 1, :]
        return carry

    lax.fori_loop(0, (count + SUB - 1) >> 3, waited, 0)
    kept = pltpu.make_async_copy(
        stayed.at[:, pl.ds(0, slots), :], parcel_out.at[:, pl.ds(0, slots), :], sems.at[5]
    )
    kept.start()
    for tail in tails:
        tail.wait()
    per_box = capacity // SUB

    def arriving(g):
        d, first = g // per_box, g % per_box * SUB
        inbox, row = inboxes[d], g * SUB
        values = [
            inbox[first + f * capacity : first + f * capacity + SUB, :]
            for f in range(FIELDS)
        ]

        def store(c, part, value):
            parcel_new[c, row : row + SUB, part] = value

        local = [
            local_of(arrived[d * SUB, row + b].astype(jnp.int32), dims)
            for b in range(SUB)
        ]
        return values[0], values[1:4], values[4], values[5], local, store

    pipeline(space, acc, arriving, 4 * per_box, width // LANES)
    fresh = pltpu.make_async_copy(
        parcel_new, parcel_out.at[:, pl.ds(slots, 4 * capacity), :], sems.at[6]
    )
    fresh.start()

    lane_row = lax.broadcasted_iota(jnp.int32, (cells_y, LANES), 1)
    pitch = chunks * SUB

    def finish(i, carry):
        for c in range(comps):
            before = jnp.zeros((cells_y, LANES), F32)
            for h in range(chunks):
                base = i * cells_y * pitch + h * SUB + c
                low = acc[pl.ds(base, cells_y, stride=pitch), :]
                high = acc[pl.ds(base + comps, cells_y, stride=pitch), :]
                turned = pltpu.roll(high, 1, 1)
                moved = jnp.where(lane_row == 0, before, turned)
                before = turned
                gas_new[c, i, :, h * LANES : (h + 1) * LANES] = (
                    field[c, h, i] + low
                ) + moved
        pltpu.make_async_copy(
            gas_new.at[:, i], gas_out.at[:, i], plane_sems.at[i]
        ).start()
        return carry

    lax.fori_loop(0, cells_x, finish, 0, unroll=True)

    def settle(i, carry):
        pltpu.make_async_copy(
            gas_new.at[:, i], gas_out.at[:, i], plane_sems.at[i]
        ).wait()
        return carry

    lax.fori_loop(0, cells_x, settle, 0)
    kept.wait()
    fresh.wait()


def neighbour(value, axis, steps):
    count = lax.axis_size(axis)
    pairs = [(source, (source + steps) % count) for source in range(count)]
    return lax.ppermute(value, axis, pairs)


def params(mib):
    return pltpu.CompilerParams(vmem_limit_bytes=mib << 20)


def step(gas_velocity, parcel_z, parcel_velocity, parcel_rate, parcel_mass, parcel_column):
    comps, cells_x, cells_y, depth = gas_velocity.shape
    slots, width = parcel_z.shape
    capacity = slots // 4
    chunks = depth // LANES
    tiles = width // LANES
    cells = cells_x * cells_y
    x_count = lax.axis_size("gx")
    y_count = lax.axis_size(Y_AXES)
    dims = (x_count, y_count, cells_x, cells_y)
    velocity = jnp.transpose(parcel_velocity, (1, 0, 2))
    struct = lambda *shape: jax.ShapeDtypeStruct(shape, F32)

    ext_shape = (comps, chunks, cells_x + 4, cells_y + 2 * SUB, LANES)
    x_up, x_down, y_up, y_down, ext, state, numbers = pl.pallas_call(
        faces_kernel,
        out_shape=(
            struct(comps, chunks, 2, cells_y, LANES),
            struct(comps, chunks, 2, cells_y, LANES),
            struct(comps, chunks, 2, cells_x, LANES),
            struct(comps, chunks, 2, cells_x, LANES),
            struct(*ext_shape),
            struct(FIELDS, slots, width),
            jax.ShapeDtypeStruct((1, slots), jnp.int32),
        ),
        in_specs=[HBM] * 6,
        out_specs=(VMEM,) * 7,
        scratch_shapes=[pltpu.SemaphoreType.DMA((chunks + 5,))],
        compiler_params=params(8),
        name="faces",
    )(
        *(
            pltpu.with_memory_space_constraint(value, pltpu.HBM)
            for value in (
                gas_velocity,
                parcel_z,
                velocity,
                parcel_rate,
                parcel_mass,
                parcel_column.reshape(1, slots),
            )
        )
    )
    x_low = neighbour(x_up, "gx", 1)
    x_high = neighbour(x_down, "gx", -1)
    y_low = neighbour(y_up, Y_AXES, 1)
    y_high = neighbour(y_down, Y_AXES, -1)

    box = struct(FIELDS * capacity + SUB, width)
    lines_in_box = -(-(1 + comps * chunks) // SUB) * SUB
    long_box = struct(FIELDS * capacity + lines_in_box, width)
    outbox = pl.pallas_call(
        functools.partial(pack_kernel, dims, capacity),
        out_shape=(
            long_box,
            long_box,
            box,
            box,
            struct(slots, LANES),
            jax.ShapeDtypeStruct((1, slots), jnp.int32),
        ),
        in_specs=[VMEM] * 2,
        out_specs=(VMEM,) * 6,
        compiler_params=params(8),
        name="pack",
    )(numbers, state)
    in2 = neighbour(outbox[2], Y_AXES, 1)
    in3 = neighbour(outbox[3], Y_AXES, -1)

    acc_struct = struct(cells * chunks * SUB, LANES)
    late, info, acc = pl.pallas_call(
        late_kernel,
        out_shape=(
            struct(FIELDS * slots, width),
            struct(SUB, max(LANES, slots)),
            acc_struct,
        ),
        in_specs=[VMEM] * 3,
        out_specs=(VMEM,) * 3,
        compiler_params=params(8),
        name="late",
    )(numbers, outbox[5], state)
    box0, box1, acc = pl.pallas_call(
        functools.partial(relay_kernel, capacity),
        out_shape=(long_box, long_box, acc_struct),
        in_specs=[VMEM] * 5,
        out_specs=(VMEM,) * 3,
        input_output_aliases={2: 0, 3: 1, 4: 2},
        compiler_params=params(8),
        name="relay",
    )(y_low, y_high, outbox[0], outbox[1], acc)
    in0 = neighbour(box0, "gx", 1)
    in1 = neighbour(box1, "gx", -1)

    steps = -(-comps * chunks // SUB)
    scratch = [
        pltpu.VMEM((2 * UNROLL, steps, SUB * SUB, LANES), F32),
        pltpu.VMEM((2 * UNROLL, tiles, 2 * SUB * SUB, LANES), F32),
        pltpu.VMEM((2 * UNROLL, tiles, 2 * SUB, LANES), F32),
    ]
    lines, acc, stayed, field, _ = pl.pallas_call(
        functools.partial(stay_kernel, dims),
        out_shape=(
            struct(cells * steps * SUB, LANES),
            acc_struct,
            struct(3, slots + SUB, width),
            struct(comps, chunks, cells_x, cells_y, LANES),
            struct(*ext_shape),
        ),
        in_specs=[SMEM] + [VMEM] * 10,
        out_specs=(VMEM,) * 5,
        scratch_shapes=[
            pltpu.VMEM((comps, chunks, cells_x + 2, cells_y + 2 * SUB, LANES), F32),
        ]
        + scratch,
        input_output_aliases={1: 4, 2: 1},
        compiler_params=params(16),
        name="stay",
    )(
        parcel_column,
        ext,
        acc,
        x_low,
        x_high,
        y_low,
        y_high,
        y_up,
        y_down,
        state,
        outbox[4],
    )
    gas_out, updated = pl.pallas_call(
        functools.partial(arrive_kernel, dims, capacity),
        out_shape=(
            struct(comps, cells_x, cells_y, depth),
            struct(3, slots + 4 * capacity, width),
            acc_struct,
            struct(cells * steps * SUB, LANES),
            struct(3, slots + SUB, width),
            struct(comps, chunks, cells_x, cells_y, LANES),
        ),
        in_specs=[VMEM] * 10,
        out_specs=(HBM, HBM) + (VMEM,) * 4,
        scratch_shapes=[
            pltpu.VMEM((comps, cells_x, cells_y, depth), F32),
            pltpu.VMEM((3, 4 * capacity, width), F32),
        ]
        + scratch
        + [
            pltpu.SMEM((4 * SUB, LANES), F32),
            pltpu.SMEM((SUB, max(LANES, slots)), F32),
            pltpu.VMEM((3, SUB, width), F32),
            pltpu.SemaphoreType.DMA((7,)),
            pltpu.SemaphoreType.DMA((cells_x,)),
        ],
        input_output_aliases={6: 3, 7: 2, 8: 4, 9: 5},
        compiler_params=params(16),
        name="arrive",
    )(in0, in1, in2, in3, late, info, lines, acc, stayed, field)[:2]
    return gas_out, jnp.transpose(updated, (1, 0, 2))


def solution(mesh):
    placed = (
        P(None, "gx", Y_AXES, None),
        P(("grp", "gx", "gy"), None),
        P(("grp", "gx", "gy"), None, None),
        P(("grp", "gx", "gy"), None),
        P(("grp", "gx", "gy"), None),
        P(("grp", "gx", "gy")),
    )
    return jax.shard_map(
        step,
        mesh=mesh,
        in_specs=placed,
        out_specs=(P(None, "gx", Y_AXES, None), P(("grp", "gx", "gy"), None, None)),
        check_vma=False,
    )
```
